128 devices in a mesh: row: 16 (over x, z_hi, core), col: 8 (over z_lo, y).
Axes of the slice: x: 4, y: 4, z: 4 (z_hi: 2, z_lo: 2; z = z_hi * 2 + z_lo), core: 2. Of those that a mesh axis runs over, the one named last changes fastest.
Arguments:
- vectors: bfloat16 [16, 262144], P(None, ('row', 'col'))
- stiffness: bfloat16 [16, 8, 192, 128, 128], P('row', 'col'), may hold values from -0.109375 to 0.109375
- block_row: int32 [16, 8, 192], P('row', 'col'), may hold values from 0 to 127
- block_col: int32 [16, 8, 192], P('row', 'col'), may hold values from 0 to 255
- block_count: int32 [16, 8], P('row', 'col'), may hold values from 1 to 192, as said below
- diag_blocks: bfloat16 [2048, 128, 128], P(('row', 'col'))
- precond: bfloat16 [2048, 128, 128], P(('row', 'col')), may hold values from -0.5 to 0.5
Outputs:
- image: float32 [16, 262144], P(None, ('row', 'col'))
- search: bfloat16 [16, 262144], P(None, ('row', 'col'))
The draws below stay inside these ranges and needn't reach their ends.
Inputs may be any that keep to these rules, and one draw needn't show every extreme that they name: block_count is at most 192 and equals 192 on at least one grid cell in every draw.
All inputs are finite; a program needn't handle non-finite values.
Results may differ from the reference program's by a relative error of at most 0.0051.
Values may be sent and summed in bfloat16 or wider, within the bound.
No kernel may reach another device: no remote copies, remote signals or barrier semaphores. Data moves between devices by JAX's collectives and lax.ppermute only.
A program may use at most 128 MiB of HBM per device.

```python
import math
import jax
import jax.numpy as jnp
from jax import lax

BLOCK = 128
WIDTH = 16
BR_DEV = 16
NB_DEV = 192
NBLK = 2048
NROWS = 262144
N_ROW = 16
N_COL = 8


def draw_vectors(key, part):
    keys = jax.random.split(key, 3)
    place = jnp.arange(NROWS, dtype=jnp.float32) / NROWS
    row_spread = jax.random.uniform(keys[1], (1, NROWS), jnp.float32)
    col_spread = jax.random.uniform(keys[2], (WIDTH, 1), jnp.float32)
    base = jax.random.normal(keys[0], (WIDTH, NROWS), jnp.float32)
    rise = math.log(3.0)
    scale = jnp.exp(rise * (place[None, :] - 0.5) + math.log(10.0) * (row_spread - 0.5) + math.log(10.0) * (col_spread - 0.5))
    return (base * scale).astype(jnp.bfloat16)


def draw_block_count(key, part):
    keys = jax.random.split(key, 2)
    shifts = jax.random.randint(keys[0], (N_ROW, N_COL), 0, 4)
    counts = jnp.maximum(jnp.right_shift(jnp.full((N_ROW, N_COL), NB_DEV, jnp.int32), shifts), 1)
    chosen = jax.random.randint(keys[1], (), 0, N_ROW * N_COL)
    counts = counts.reshape(-1).at[chosen].set(NB_DEV)
    return counts.reshape(N_ROW, N_COL).astype(jnp.int32)


def draw_diag_blocks(key, part):
    keys = jax.random.split(key, 2)
    rows_i = jnp.arange(BLOCK)[:, None]
    cols_i = jnp.arange(BLOCK)[None, :]
    on_diag = (rows_i == cols_i)[None, :, :]
    diag_vals = jnp.exp(jax.random.uniform(keys[0], (NBLK, BLOCK, 1), jnp.float32) * math.log(4.0))
    off = jax.random.normal(keys[1], (NBLK, BLOCK, BLOCK), jnp.float32) / math.sqrt(BLOCK)
    return jnp.where(on_diag, diag_vals, off).astype(jnp.bfloat16)


def touch_ends(array, key, least, top_value):
    spot = [jax.random.randint(jax.random.fold_in(key, axis), (), 0, length) for axis, length in enumerate(array.shape)]
    widest = array.shape.index(max(array.shape))
    next_to = spot[:widest] + [(spot[widest] + 1) % array.shape[widest]] + spot[widest + 1:]
    return array.at[tuple(spot)].set(least).at[tuple(next_to)].set(top_value)


def level_of(key, extent, cuts, low, top_value):
    loudness, own = 1.0, jax.random.fold_in(key, 6)
    for position, parts in cuts:
        steps = jnp.exp(jax.random.uniform(jax.random.fold_in(own, position), (parts,), jnp.float32, low / len(cuts), top_value / len(cuts)))
        loudness = loudness * jnp.repeat(steps, extent[position] // parts).reshape([-1 if axis == position else 1 for axis in range(len(extent))])
    return loudness


def centred(key, extent, width, bound, cuts=(), kind=jnp.bfloat16):
    drawn = width * jax.random.normal(key, extent, jnp.float32)
    if cuts:
        drawn = drawn * level_of(key, extent, cuts, -0.22, 0.18)
    return jnp.clip(drawn, -bound, bound).astype(kind)


def setup_inputs(seed: int = 0) -> dict:
    splits = jax.random.split(jax.random.key(seed), 8)
    return {
        "vectors": draw_vectors(jax.random.fold_in(splits[7], 71), 0),
        "stiffness": centred(splits[1], (N_ROW, N_COL, NB_DEV, BLOCK, BLOCK), (256 * NB_DEV // BR_DEV) ** -0.5, 0.109375, ((0, 16), (1, 8))),
        "block_row": touch_ends(jax.random.randint(splits[2], (N_ROW, N_COL, NB_DEV), 0, N_COL * BR_DEV), jax.random.fold_in(splits[2], 1), 0, (N_COL * BR_DEV) - 1).astype(jnp.int32),
        "block_col": touch_ends(jax.random.randint(splits[3], (N_ROW, N_COL, NB_DEV), 0, N_ROW * BR_DEV), jax.random.fold_in(splits[3], 1), 0, (N_ROW * BR_DEV) - 1).astype(jnp.int32),
        "block_count": draw_block_count(jax.random.fold_in(splits[7], 71), 0),
        "diag_blocks": draw_diag_blocks(jax.random.fold_in(splits[7], 71), 0),
        "precond": centred(splits[6], (NBLK, BLOCK, BLOCK), BLOCK ** -0.5, 0.5, ((0, 128),)),
    }


def reference(vectors, stiffness, block_row, block_col, block_count, diag_blocks, precond):
    vec_count = vectors.shape[0]
    split_vec = vectors.reshape(vec_count, NBLK, BLOCK).astype(jnp.float32)
    grid_rows = jnp.arange(N_ROW, dtype=jnp.int32)[:, None, None]
    grid_cols = jnp.arange(N_COL, dtype=jnp.int32)[None, :, None]
    global_row = (grid_rows * (N_COL * BR_DEV) + block_row).astype(jnp.int32)
    global_col = ((block_col // BR_DEV) * (N_COL * BR_DEV) + grid_cols * BR_DEV + block_col % BR_DEV).astype(jnp.int32)
    live_mask = (jnp.arange(NB_DEV, dtype=jnp.int32)[None, None, :] < block_count[:, :, None]).astype(jnp.float32)
    cells = N_ROW * N_COL
    items = (stiffness.reshape(cells, NB_DEV, BLOCK, BLOCK), global_row.reshape(cells, NB_DEV),
             global_col.reshape(cells, NB_DEV), live_mask.reshape(cells, NB_DEV))

    def one_cell(carry, item):
        blocks, rows_at, cols_at, live = item
        blocks_f = blocks.astype(jnp.float32)
        to_row = jnp.einsum('knb,nab->kna', split_vec[:, cols_at], blocks_f) * live[None, :, None]
        to_col = jnp.einsum('kna,nab->knb', split_vec[:, rows_at], blocks_f) * live[None, :, None]
        carry = carry.at[:, rows_at].add(to_row)
        carry = carry.at[:, cols_at].add(to_col)
        return carry, None

    start = jnp.zeros((vec_count, NBLK, BLOCK), jnp.float32)
    summed, unused = lax.scan(one_cell, start, items)
    diag_f = diag_blocks.astype(jnp.float32)
    summed = summed + jnp.einsum('nab,knb->kna', diag_f, split_vec) + jnp.einsum('nba,knb->kna', diag_f, split_vec)
    image = summed.reshape(vec_count, NROWS)
    vectors_f = vectors.astype(jnp.float32)
    lengths = jnp.sum(vectors_f * vectors_f, axis=1)
    inner = jnp.sum(vectors_f * image, axis=1)
    theta = inner / lengths
    resid = (image - theta[:, None] * vectors_f).astype(jnp.bfloat16)
    resid_f = resid.reshape(vec_count, NBLK, BLOCK).astype(jnp.float32)
    search = jnp.einsum('nab,knb->kna', precond.astype(jnp.float32), resid_f)
    return image, search.reshape(vec_count, NROWS).astype(jnp.bfloat16)
```

```python
import functools
import jax
import jax.numpy as jnp
from jax import lax
from jax.experimental import pallas as pl
from jax.experimental.pallas import tpu as pltpu
from jax.sharding import PartitionSpec as P

CHUNK = 16
GROUP = 8
LANES = 128
F32 = jnp.float32
BF16 = jnp.bfloat16


def split_tile(xy, xx, width):
    lane = lax.broadcasted_iota(jnp.int32, (width, LANES), 1)
    v = jnp.where(lane % 2 == 0, xy, xx)
    hi = v.astype(BF16).astype(F32)
    mid = (v - hi).astype(BF16).astype(F32)
    low = v - hi - mid
    tile = jnp.where(lane < 2, hi, jnp.where(lane < 4, mid, jnp.where(lane < 6, low, 0.0)))
    return tile.astype(BF16)


def join_tile(tile):
    lane = lax.broadcasted_iota(jnp.int32, tile.shape, 1)
    xy = jnp.sum(jnp.where(lane % 2 == 0, tile, 0.0), axis=1, keepdims=True)
    xx = jnp.sum(jnp.where(lane % 2 == 1, tile, 0.0), axis=1, keepdims=True)
    return xy, xx


def block_kernel(count_ref, rows_ref, cols_ref, x_ref, xrow_ref, xcol_ref, diag_ref, stiff_ref,
                 out_row, out_col, out_diag, acc_row, acc_col, buf, sems):
    slots = stiff_ref.shape[0]
    chunks = slots // CHUNK
    n_row, width, span = xrow_ref.shape
    n_col = xcol_ref.shape[0]
    owned = span // LANES
    copies = [
        pltpu.make_async_copy(stiff_ref.at[pl.ds(c * CHUNK, CHUNK)], buf.at[pl.ds(c * CHUNK, CHUNK)], sems.at[c])
        for c in range(chunks)
    ]
    for copy in copies:
        copy.start()
    acc_row[...] = jnp.zeros_like(acc_row)
    acc_col[...] = jnp.zeros_like(acc_col)
    xy = jnp.zeros((width, LANES), F32)
    xx = jnp.zeros((width, LANES), F32)
    for g in range(owned):
        here = slice(g * LANES, (g + 1) * LANES)
        xg = x_ref[:, here]
        d = diag_ref[g]
        term = lax.dot_general(xg, d, (((1,), (1,)), ((), ())), preferred_element_type=F32)
        term = term + lax.dot_general(xg, d, (((1,), (0,)), ((), ())), preferred_element_type=F32)
        out_diag[:, here] = term
        xf = xg.astype(F32)
        xy = xy + xf * term
        xx = xx + xf * xf
    count = count_ref[0]
    for c in range(chunks):
        copies[c].wait()

        @pl.when(c * CHUNK < count)
        def _():
            for h in range(CHUNK // GROUP):
                found = []
                for u in range(GROUP):
                    n = c * CHUNK + h * GROUP + u
                    i = rows_ref[n]
                    j = cols_ref[n]
                    b = buf[n]
                    xc = xcol_ref[j // owned, :, pl.ds(pl.multiple_of((j % owned) * LANES, LANES), LANES)]
                    xr = xrow_ref[i // owned, :, pl.ds(pl.multiple_of((i % owned) * LANES, LANES), LANES)]
                    to_row = lax.dot_general(xc, b, (((1,), (1,)), ((), ())), preferred_element_type=F32)
                    to_col = lax.dot_general(xr, b, (((1,), (0,)), ((), ())), preferred_element_type=F32)
                    live = n < count
                    found.append((jnp.where(live, i, n_row * owned), jnp.where(live, j, n_col * owned), to_row, to_col))
                for i, j, to_row, to_col in found:
                    acc_row[i] += to_row
                    acc_col[j] += to_col

    part = jnp.zeros((width, LANES), F32)
    for d in range(n_row):
        for t in range(owned):
            here = slice(t * LANES, (t + 1) * LANES)
            a = acc_row[d * owned + t]
            part = part + a * xrow_ref[d, :, here].astype(F32)
            out_row[d, :, here] = a.astype(BF16)
    xy = jnp.sum(xy + 2.0 * part, axis=1, keepdims=True)
    xx = jnp.sum(xx, axis=1, keepdims=True)
    tile = split_tile(xy, xx, width)
    for d in range(n_col):
        for t in range(owned):
            out_col[d, :, t * LANES:(t + 1) * LANES] = acc_col[d * owned + t].astype(BF16)
        out_col[d, :, span:] = tile
    for d in range(n_row):
        out_row[d, :, span:] = tile


def middle_kernel(col_ref, diag_ref, row_in, sum_ref, row_ref):
    n_col, width, wide = col_ref.shape
    span = wide - LANES
    for t in range(span // LANES):
        here = slice(t * LANES, (t + 1) * LANES)
        total = diag_ref[:, here]
        for d in range(n_col):
            total = total + col_ref[d, :, here].astype(F32)
        sum_ref[:, here] = total
    tile = col_ref[0, :, span:].astype(F32)
    for d in range(1, n_col):
        tile = tile + col_ref[d, :, span:].astype(F32)
    xy, xx = join_tile(tile)
    out = split_tile(xy, xx, width)
    for d in range(row_ref.shape[0]):
        row_ref[d, :, :span] = row_in[d, :, :span]
        row_ref[d, :, span:] = out


def final_kernel(row_ref, sum_ref, x_ref, pre_ref, image_ref, search_ref):
    n_row, width, wide = row_ref.shape
    span = wide - LANES
    tile = row_ref[0, :, span:].astype(F32)
    for d in range(1, n_row):
        tile = tile + row_ref[d, :, span:].astype(F32)
    xy, xx = join_tile(tile)
    theta = xy / xx
    for t in range(span // LANES):
        here = slice(t * LANES, (t + 1) * LANES)
        total = sum_ref[:, here]
        for d in range(n_row):
            total = total + row_ref[d, :, here].astype(F32)
        image_ref[:, here] = total
        resid = (total - theta * x_ref[:, here].astype(F32)).astype(BF16)
        out = lax.dot_general(resid, pre_ref[t], (((1,), (1,)), ((), ())), preferred_element_type=F32)
        search_ref[:, here] = out.astype(BF16)


VM = pl.BlockSpec(memory_space=pltpu.VMEM)
SM = pl.BlockSpec(memory_space=pltpu.SMEM)


def spread(x, axis, count):
    return lax.all_to_all(jnp.broadcast_to(x[None], (count, *x.shape)), axis, 0, 0, tiled=True)


def per_device(vectors, stiffness, block_row, block_col, block_count, diag_blocks, precond):
    width, span = vectors.shape
    owned, block_len, _ = diag_blocks.shape
    slots = stiffness.shape[2]
    row_devs = lax.axis_size("row")
    col_devs = lax.axis_size("col")
    xrow = spread(vectors, "col", col_devs)
    xcol = spread(vectors, "row", row_devs)
    wide = span + LANES
    out_row, out_col, diag_term = pl.pallas_call(
        block_kernel,
        out_shape=(
            jax.ShapeDtypeStruct((col_devs, width, wide), BF16),
            jax.ShapeDtypeStruct((row_devs, width, wide), BF16),
            jax.ShapeDtypeStruct((width, span), F32),
        ),
        in_specs=[SM, SM, SM, VM, VM, VM, VM, pl.BlockSpec(memory_space=pl.ANY)],
        out_specs=(VM, VM, VM),
        scratch_shapes=[
            pltpu.VMEM((col_devs * owned + 1, width, LANES), F32),
            pltpu.VMEM((row_devs * owned + 1, width, LANES), F32),
            pltpu.VMEM((slots, block_len, block_len), BF16),
            pltpu.SemaphoreType.DMA((slots // CHUNK,)),
        ],
        compiler_params=pltpu.CompilerParams(vmem_limit_bytes=40 << 20),
    )(block_count.reshape(1), block_row.reshape(slots), block_col.reshape(slots), vectors, xrow, xcol,
      diag_blocks, stiffness.reshape(slots, block_len, block_len))
    got_col = lax.all_to_all(out_col, "row", 0, 0, tiled=True)
    part, out_row = pl.pallas_call(
        middle_kernel,
        out_shape=(jax.ShapeDtypeStruct((width, span), F32), jax.ShapeDtypeStruct((col_devs, width, wide), BF16)),
        in_specs=[VM] * 3,
        out_specs=(VM, VM),
        compiler_params=pltpu.CompilerParams(vmem_limit_bytes=24 << 20),
    )(got_col, diag_term, out_row)
    got_row = lax.all_to_all(out_row, "col", 0, 0, tiled=True)
    return pl.pallas_call(
        final_kernel,
        out_shape=(jax.ShapeDtypeStruct((width, span), F32), jax.ShapeDtypeStruct((width, span), BF16)),
        in_specs=[VM] * 4,
        out_specs=(VM, VM),
        compiler_params=pltpu.CompilerParams(vmem_limit_bytes=24 << 20),
    )(got_row, part, vectors, precond)


def solution(mesh):
    placed = (
        P(None, ("row", "col")),
        P("row", "col", None, None, None),
        P("row", "col", None),
        P("row", "col", None),
        P("row", "col"),
        P(("row", "col"), None, None),
        P(("row", "col"), None, None),
    )
    return jax.shard_map(
        per_device,
        mesh=mesh,
        in_specs=placed,
        out_specs=(P(None, ("row", "col")), P(None, ("row", "col"))),
        check_vma=False,
    )
```

```python
import functools
import jax
import jax.numpy as jnp
from jax import lax
from jax.experimental import pallas as pl
from jax.experimental.pallas import tpu as pltpu
from jax.sharding import PartitionSpec as P

CHUNK = 16
LANES = 128
F32 = jnp.float32
BF16 = jnp.bfloat16


def split_tile(xy, xx, width):
    lane = lax.broadcasted_iota(jnp.int32, (width, LANES), 1)
    v = jnp.where(lane % 2 == 0, xy, xx)
    hi = v.astype(BF16).astype(F32)
    mid = (v - hi).astype(BF16).astype(F32)
    low = v - hi - mid
    tile = jnp.where(lane < 2, hi, jnp.where(lane < 4, mid, jnp.where(lane < 6, low, 0.0)))
    return tile.astype(BF16)


def join_tile(tile):
    lane = lax.broadcasted_iota(jnp.int32, tile.shape, 1)
    xy = jnp.sum(jnp.where(lane % 2 == 0, tile, 0.0), axis=1, keepdims=True)
    xx = jnp.sum(jnp.where(lane % 2 == 1, tile, 0.0), axis=1, keepdims=True)
    return xy, xx


def fetch(stiff_ref, buf, sems, count):
    copies = []
    for c in range(stiff_ref.shape[0] // CHUNK):
        here = pl.ds(c * CHUNK, CHUNK)
        copies.append(pltpu.make_async_copy(stiff_ref.at[here], buf.at[here], sems.at[c]))
    for c, copy in enumerate(copies):
        pl.when(c * CHUNK < count)(copy.start)
    return copies


def pair_products(xa, xb, blocks, turned):
    none = jnp.zeros_like(xa)
    x = jnp.concatenate([jnp.concatenate([xa, none], axis=1), jnp.concatenate([none, xb], axis=1)], axis=0)
    if turned:
        b = jnp.concatenate([blocks[0], blocks[1]], axis=1)
        dims = ((1,), (1,))
    else:
        b = blocks.reshape(2 * blocks.shape[1], blocks.shape[2])
        dims = ((1,), (0,))
    out = lax.dot_general(x, b, (dims, ((), ())), preferred_element_type=F32)
    return out[:xa.shape[0]], out[xa.shape[0]:]


def add_blocks(copies, count, take_ref, give_ref, x_blocks, turned, buf, acc):
    spare = acc.shape[0] - 1
    for c, copy in enumerate(copies):

        @pl.when(c * CHUNK < count)
        def _():
            copy.wait()
            found = []
            for n in range(c * CHUNK, (c + 1) * CHUNK, 2):
                terms = pair_products(x_blocks[take_ref[n]], x_blocks[take_ref[n + 1]], buf[n:n + 2], turned)
                for k in range(2):
                    found.append((jnp.where(n + k < count, give_ref[n + k], spare), terms[k]))
            for g, term in found:
                acc[g] += term


def first_kernel(count_ref, rows_ref, cols_ref, x_ref, z_ref, *refs):
    (*pair_refs, diag_ref, stiff_ref, out_col, out_diag, x_row, acc, buf, sems) = refs
    copies = fetch(stiff_ref, buf, sems, count_ref[0, 0])
    width, span = x_ref.shape
    owned = span // LANES
    runs = len(pair_refs) + 1
    place = lax.axis_index("col")
    zl = place // runs
    y = place % runs
    for s in range(runs):
        for k in range(2):
            dev = ((zl + k) % 2) * runs + (y + runs - s) % runs
            for t in range(owned):
                here = slice(t * LANES, (t + 1) * LANES)
                piece = (x_ref if k == 0 else z_ref)[:, here] if s == 0 else pair_refs[s - 1][k, :, here]
                x_row[dev * owned + t] = piece
    acc[...] = jnp.zeros_like(acc)
    for g in range(owned):
        here = slice(g * LANES, (g + 1) * LANES)
        xg = x_ref[:, here]
        d = diag_ref[g]
        term = lax.dot_general(xg, d, (((1,), (1,)), ((), ())), preferred_element_type=F32)
        out_diag[:, here] = term + lax.dot_general(xg, d, (((1,), (0,)), ((), ())), preferred_element_type=F32)
    add_blocks(copies, count_ref[0, 0], rows_ref, cols_ref, x_row, False, buf, acc)
    for d in range(out_col.shape[0]):
        for t in range(owned):
            out_col[d, :, t * LANES:(t + 1) * LANES] = acc[d * owned + t].astype(BF16)


def second_kernel(count_ref, rows_ref, cols_ref, x_ref, diag_ref, x_row, xcol_ref, stiff_ref, col_in,
                  out_row, out_col, x_col, acc, buf, sems):
    copies = fetch(stiff_ref, buf, sems, count_ref[0, 0])
    width, span = x_ref.shape
    owned = span // LANES
    for d in range(xcol_ref.shape[0]):
        for t in range(owned):
            x_col[d * owned + t] = xcol_ref[d, :, t * LANES:(t + 1) * LANES]
    acc[...] = jnp.zeros_like(acc)
    add_blocks(copies, count_ref[0, 0], cols_ref, rows_ref, x_col, True, buf, acc)
    part = jnp.zeros((width, LANES), F32)
    for d in range(out_row.shape[0]):
        for t in range(owned):
            a = acc[d * owned + t]
            part = part + a * x_row[d * owned + t].astype(F32)
            out_row[d, :, t * LANES:(t + 1) * LANES] = a.astype(BF16)
    xy = 2.0 * part
    xx = jnp.zeros((width, LANES), F32)
    for t in range(owned):
        here = slice(t * LANES, (t + 1) * LANES)
        xf = x_ref[:, here].astype(F32)
        xy = xy + xf * diag_ref[:, here]
        xx = xx + xf * xf
    tile = split_tile(jnp.sum(xy, axis=1, keepdims=True), jnp.sum(xx, axis=1, keepdims=True), width)
    for d in range(out_col.shape[0]):
        out_col[d, :, :span] = col_in[d]
        out_col[d, :, span:] = tile


def pair_kernel(x_ref, z_ref, many_in, out_ref, many_ref):
    out_ref[0] = x_ref[...]
    out_ref[1] = z_ref[...]


def copies_kernel(x_ref, out_ref):
    for d in range(out_ref.shape[0]):
        out_ref[d] = x_ref[...]


def middle_kernel(col_ref, diag_ref, row_in, sum_ref, row_ref):
    n_col, width, wide = col_ref.shape
    span = wide - LANES
    for t in range(span // LANES):
        here = slice(t * LANES, (t + 1) * LANES)
        total = diag_ref[:, here]
        for d in range(n_col):
            total = total + col_ref[d, :, here].astype(F32)
        sum_ref[:, here] = total
    tile = col_ref[0, :, span:].astype(F32)
    for d in range(1, n_col):
        tile = tile + col_ref[d, :, span:].astype(F32)
    xy, xx = join_tile(tile)
    out = split_tile(xy, xx, width)
    for d in range(row_ref.shape[0]):
        row_ref[d, :, :span] = row_in[d]
        row_ref[d, :, span:] = out


def final_kernel(row_ref, sum_ref, x_ref, pre_ref, image_ref, search_ref):
    n_row, width, wide = row_ref.shape
    span = wide - LANES
    tile = row_ref[0, :, span:].astype(F32)
    for d in range(1, n_row):
        tile = tile + row_ref[d, :, span:].astype(F32)
    xy, xx = join_tile(tile)
    theta = xy / xx
    for t in range(span // LANES):
        here = slice(t * LANES, (t + 1) * LANES)
        total = sum_ref[:, here]
        for d in range(n_row):
            total = total + row_ref[d, :, here].astype(F32)
        image_ref[:, here] = total
        resid = (total - theta * x_ref[:, here].astype(F32)).astype(BF16)
        out = lax.dot_general(resid, pre_ref[t], (((1,), (1,)), ((), ())), preferred_element_type=F32)
        search_ref[:, here] = out.astype(BF16)


VM = pl.BlockSpec(memory_space=pltpu.VMEM)
SM = pl.BlockSpec(memory_space=pltpu.SMEM)
ANY = pl.BlockSpec(memory_space=pl.ANY)
HBM = pl.BlockSpec(memory_space=pltpu.HBM)


def near(x):
    return pltpu.with_memory_space_constraint(x, pltpu.VMEM)


def params(mib):
    return pltpu.CompilerParams(vmem_limit_bytes=mib << 20)


def cost(flops, moved):
    return pl.CostEstimate(flops=flops, bytes_accessed=moved, transcendentals=0)


def per_device(vectors, stiffness, block_row, block_col, block_count, diag_blocks, precond):
    width, span = vectors.shape
    owned, block_len, _ = diag_blocks.shape
    slots = stiffness.shape[2]
    row_devs = lax.axis_size("row")
    col_devs = lax.axis_size("col")
    runs = col_devs // 2
    wide = span + LANES
    count = block_count
    rows = block_row.reshape(slots)
    cols = block_col.reshape(slots)
    block_scratch = [pltpu.VMEM((slots, block_len, block_len), BF16), pltpu.SemaphoreType.DMA((slots // CHUNK,))]
    blocks = pltpu.with_memory_space_constraint(stiffness.reshape(slots, block_len, block_len), pltpu.HBM)

    beside = near(lax.ppermute(vectors, "col", [(i, (i + runs) % col_devs) for i in range(col_devs)]))
    many = pl.pallas_call(
        copies_kernel,
        out_shape=jax.ShapeDtypeStruct((row_devs, width, span), BF16),
        in_specs=[VM],
        out_specs=VM,
        cost_estimate=cost(0, 4 << 20),
    )(vectors)
    pair, many = pl.pallas_call(
        pair_kernel,
        out_shape=(
            jax.ShapeDtypeStruct((2, width, span), BF16),
            jax.ShapeDtypeStruct((row_devs, width, span), BF16),
        ),
        in_specs=[VM, VM, ANY],
        out_specs=(VM, ANY),
        input_output_aliases={2: 1},
    )(vectors, beside, many)
    pair = near(pair)
    xcol = lax.all_to_all(many, "row", 0, 0, tiled=True)
    turned = [
        near(lax.ppermute(pair, "col", [(i, i // runs * runs + (i + s) % runs) for i in range(col_devs)]))
        for s in range(1, runs)
    ]
    out_col, diag_term, x_row = pl.pallas_call(
        first_kernel,
        out_shape=(
            jax.ShapeDtypeStruct((row_devs, width, span), BF16),
            jax.ShapeDtypeStruct((width, span), F32),
            jax.ShapeDtypeStruct((col_devs * owned, width, LANES), BF16),
        ),
        in_specs=[SM] * 3 + [VM] * (runs + 2) + [HBM],
        out_specs=(VM, VM, VM),
        scratch_shapes=[pltpu.VMEM((row_devs * owned + 1, width, LANES), F32)] + block_scratch,
        compiler_params=params(24),
        cost_estimate=cost(4 << 30, 8 << 20),
    )(count, rows, cols, vectors, beside, *turned, diag_blocks, blocks)
    out_row, out_col = pl.pallas_call(
        second_kernel,
        out_shape=(
            jax.ShapeDtypeStruct((col_devs, width, span), BF16),
            jax.ShapeDtypeStruct((row_devs, width, wide), BF16),
        ),
        in_specs=[SM] * 3 + [VM] * 4 + [HBM, VM],
        out_specs=(VM, VM),
        scratch_shapes=[
            pltpu.VMEM((row_devs * owned, width, LANES), BF16),
            pltpu.VMEM((col_devs * owned + 1, width, LANES), F32),
        ] + block_scratch,
        compiler_params=params(24),
    )(count, rows, cols, vectors, diag_term, x_row, xcol, blocks, out_col)
    got_col = lax.all_to_all(out_col, "row", 0, 0, tiled=True)
    part, out_row = pl.pallas_call(
        middle_kernel,
        out_shape=(jax.ShapeDtypeStruct((width, span), F32), jax.ShapeDtypeStruct((col_devs, width, wide), BF16)),
        in_specs=[VM] * 3,
        out_specs=(VM, VM),
        compiler_params=params(16),
    )(got_col, diag_term, out_row)
    got_row = lax.all_to_all(out_row, "col", 0, 0, tiled=True)
    return pl.pallas_call(
        final_kernel,
        out_shape=(jax.ShapeDtypeStruct((width, span), F32), jax.ShapeDtypeStruct((width, span), BF16)),
        in_specs=[VM] * 4,
        out_specs=(VM, VM),
        compiler_params=params(16),
    )(got_row, part, vectors, precond)


def solution(mesh):
    placed = (
        P(None, ("row", "col")),
        P("row", "col", None, None, None),
        P("row", "col", None),
        P("row", "col", None),
        P("row", "col"),
        P(("row", "col"), None, None),
        P(("row", "col"), None, None),
    )
    return jax.shard_map(
        per_device,
        mesh=mesh,
        in_specs=placed,
        out_specs=(P(None, ("row", "col")), P(None, ("row", "col"))),
        check_vma=False,
    )
```

```python
import functools
import jax
import jax.numpy as jnp
from jax import lax
from jax.experimental import pallas as pl
from jax.experimental.pallas import tpu as pltpu
from jax.sharding import PartitionSpec as P

CHUNK = 16
GROUP = 8
LANES = 128
F32 = jnp.float32
BF16 = jnp.bfloat16


def split_tile(xy, xx, width):
    lane = lax.broadcasted_iota(jnp.int32, (width, LANES), 1)
    v = jnp.where(lane % 2 == 0, xy, xx)
    hi = v.astype(BF16).astype(F32)
    mid = (v - hi).astype(BF16).astype(F32)
    low = v - hi - mid
    tile = jnp.where(lane < 2, hi, jnp.where(lane < 4, mid, jnp.where(lane < 6, low, 0.0)))
    return tile.astype(BF16)


def join_tile(tile):
    lane = lax.broadcasted_iota(jnp.int32, tile.shape, 1)
    xy = jnp.sum(jnp.where(lane % 2 == 0, tile, 0.0), axis=1, keepdims=True)
    xx = jnp.sum(jnp.where(lane % 2 == 1, tile, 0.0), axis=1, keepdims=True)
    return xy, xx


def fetch(stiff_ref, buf, sems, count):
    copies = []
    for c in range(stiff_ref.shape[0] // CHUNK):
        here = pl.ds(c * CHUNK, CHUNK)
        copies.append(pltpu.make_async_copy(stiff_ref.at[here], buf.at[here], sems.at[c]))
    for c, copy in enumerate(copies):
        pl.when(c * CHUNK < count)(copy.start)
    return copies


def pair_products(xa, xb, blocks, turned):
    none = jnp.zeros_like(xa)
    x = jnp.concatenate([jnp.concatenate([xa, none], axis=1), jnp.concatenate([none, xb], axis=1)], axis=0)
    if turned:
        b = jnp.concatenate([blocks[0], blocks[1]], axis=1)
        dims = ((1,), (1,))
    else:
        b = blocks.reshape(2 * blocks.shape[1], blocks.shape[2])
        dims = ((1,), (0,))
    out = lax.dot_general(x, b, (dims, ((), ())), preferred_element_type=F32)
    return out[:xa.shape[0]], out[xa.shape[0]:]


def diag_kernel(x_ref, diag_ref, term_ref, stats_ref):
    width, span = x_ref.shape
    xy = jnp.zeros((width, LANES), F32)
    xx = jnp.zeros((width, LANES), F32)
    for g in range(span // LANES):
        here = slice(g * LANES, (g + 1) * LANES)
        xg = x_ref[:, here]
        d = diag_ref[g]
        term = lax.dot_general(xg, d, (((1,), (1,)), ((), ())), preferred_element_type=F32)
        term = term + lax.dot_general(xg, d, (((1,), (0,)), ((), ())), preferred_element_type=F32)
        term_ref[:, here] = term
        xf = xg.astype(F32)
        xy = xy + xf * term
        xx = xx + xf * xf
    stats_ref[0] = xy
    stats_ref[1] = xx


def rows_kernel(x_ref, z_ref, *refs):
    (*pair_refs, after_ref, x_row) = refs
    owned = x_ref.shape[1] // LANES
    runs = len(pair_refs) + 1
    place = lax.axis_index("col")
    zl = place // runs
    y = place % runs
    for s in range(runs):
        for k in range(2):
            dev = ((zl + k) % 2) * runs + (y + runs - s) % runs
            for t in range(owned):
                here = slice(t * LANES, (t + 1) * LANES)
                piece = (x_ref if k == 0 else z_ref)[:, here] if s == 0 else pair_refs[s - 1][k, :, here]
                x_row[dev * owned + t] = piece


def block_kernel(count_ref, rows_ref, cols_ref, x_row, xcol_ref, twin_ref, stats_ref, stiff_ref,
                 out_row, out_col, x_col, acc_row, acc_col, buf, sems):
    count = count_ref[0, 0]
    copies = fetch(stiff_ref, buf, sems, count)
    width, span = xcol_ref.shape[2:]
    owned = span // LANES
    acc_row[...] = jnp.zeros_like(acc_row)
    acc_col[...] = jnp.zeros_like(acc_col)
    place = lax.axis_index("row")
    high = (place // 2) % 2
    core = place % 2
    for line in range(xcol_ref.shape[0]):
        for k in range(2):
            for ref, twin in ((xcol_ref, 0), (twin_ref, 1)):
                dev = line * 4 + (high + k) % 2 * 2 + (core + twin) % 2
                for t in range(owned):
                    x_col[dev * owned + t] = ref[line, k, :, t * LANES:(t + 1) * LANES]
    for c, copy in enumerate(copies):

        @pl.when(c * CHUNK < count)
        def _():
            copy.wait()
            for h in range(0, CHUNK, GROUP):
                found = []
                for n in range(c * CHUNK + h, c * CHUNK + h + GROUP, 2):
                    i = [rows_ref[n + k] for k in range(2)]
                    j = [cols_ref[n + k] for k in range(2)]
                    to_row = pair_products(x_col[j[0]], x_col[j[1]], buf[n:n + 2], True)
                    to_col = pair_products(x_row[i[0]], x_row[i[1]], buf[n:n + 2], False)
                    for k in range(2):
                        live = n + k < count
                        found.append((acc_row, jnp.where(live, i[k], acc_row.shape[0] - 1), to_row[k]))
                        found.append((acc_col, jnp.where(live, j[k], acc_col.shape[0] - 1), to_col[k]))
                for acc, g, term in found:
                    acc[g] += term

    part = jnp.zeros((width, LANES), F32)
    for d in range(out_row.shape[0]):
        for t in range(owned):
            a = acc_row[d * owned + t]
            part = part + a * x_row[d * owned + t].astype(F32)
            out_row[d, :, t * LANES:(t + 1) * LANES] = a.astype(BF16)
    xy = 2.0 * part + stats_ref[0]
    tile = split_tile(
        jnp.sum(xy, axis=1, keepdims=True), jnp.sum(stats_ref[1], axis=1, keepdims=True), width
    )
    for d in range(out_col.shape[0]):
        for t in range(owned):
            out_col[d, :, t * LANES:(t + 1) * LANES] = acc_col[d * owned + t].astype(BF16)
        out_col[d, :, span:] = tile


def middle_kernel(col_ref, diag_ref, row_in, sum_ref, row_ref):
    n_col, width, wide = col_ref.shape
    span = wide - LANES
    for t in range(span // LANES):
        here = slice(t * LANES, (t + 1) * LANES)
        total = diag_ref[:, here]
        for d in range(n_col):
            total = total + col_ref[d, :, here].astype(F32)
        sum_ref[:, here] = total
    tile = col_ref[0, :, span:].astype(F32)
    for d in range(1, n_col):
        tile = tile + col_ref[d, :, span:].astype(F32)
    xy, xx = join_tile(tile)
    out = split_tile(xy, xx, width)
    for d in range(row_ref.shape[0]):
        row_ref[d, :, :span] = row_in[d]
        row_ref[d, :, span:] = out


def final_kernel(row_ref, sum_ref, x_ref, pre_ref, image_ref, search_ref):
    n_row, width, wide = row_ref.shape
    span = wide - LANES
    tile = row_ref[0, :, span:].astype(F32)
    for d in range(1, n_row):
        tile = tile + row_ref[d, :, span:].astype(F32)
    xy, xx = join_tile(tile)
    theta = xy / xx
    for t in range(span // LANES):
        here = slice(t * LANES, (t + 1) * LANES)
        total = sum_ref[:, here]
        for d in range(n_row):
            total = total + row_ref[d, :, here].astype(F32)
        image_ref[:, here] = total
        resid = (total - theta * x_ref[:, here].astype(F32)).astype(BF16)
        out = lax.dot_general(resid, pre_ref[t], (((1,), (1,)), ((), ())), preferred_element_type=F32)
        search_ref[:, here] = out.astype(BF16)


def prepare_kernel(x_ref, z_ref, h_ref, pair_ref, lines_ref):
    pair_ref[0] = x_ref[...]
    pair_ref[1] = z_ref[...]
    for d in range(lines_ref.shape[0]):
        lines_ref[d, 0] = x_ref[...]
        lines_ref[d, 1] = h_ref[...]


VM = pl.BlockSpec(memory_space=pltpu.VMEM)
SM = pl.BlockSpec(memory_space=pltpu.SMEM)
ANY = pl.BlockSpec(memory_space=pl.ANY)
HBM = pl.BlockSpec(memory_space=pltpu.HBM)


def near(x):
    return pltpu.with_memory_space_constraint(x, pltpu.VMEM)


def params(mib):
    return pltpu.CompilerParams(vmem_limit_bytes=mib << 20)


def cost(flops, moved):
    return pl.CostEstimate(flops=flops, bytes_accessed=moved, transcendentals=0)


def per_device(vectors, stiffness, block_row, block_col, block_count, diag_blocks, precond):
    width, span = vectors.shape
    owned, block_len, _ = diag_blocks.shape
    slots = stiffness.shape[2]
    row_devs = lax.axis_size("row")
    col_devs = lax.axis_size("col")
    runs = col_devs // 2
    wide = span + LANES
    count = block_count
    rows = block_row.reshape(slots)
    cols = block_col.reshape(slots)
    block_scratch = [pltpu.VMEM((slots, block_len, block_len), BF16), pltpu.SemaphoreType.DMA((slots // CHUNK,))]
    blocks = pltpu.with_memory_space_constraint(stiffness.reshape(slots, block_len, block_len), pltpu.HBM)

    beside = near(lax.ppermute(vectors, "col", [(i, (i + runs) % col_devs) for i in range(col_devs)]))
    above = near(lax.ppermute(vectors, "row", [(i, i ^ 2) for i in range(row_devs)]))
    lines = row_devs // 4
    pair, spread = pl.pallas_call(
        prepare_kernel,
        out_shape=(
            jax.ShapeDtypeStruct((2, width, span), BF16),
            jax.ShapeDtypeStruct((lines, 2, width, span), BF16),
        ),
        in_specs=[VM, VM, VM],
        out_specs=(VM, VM),
        compiler_params=params(4),
    )(vectors, beside, above)
    pair = near(pair)
    same_line = [[x * 4 + k for x in range(lines)] for k in range(4)]
    xcol = lax.all_to_all(spread, "row", 0, 0, axis_index_groups=same_line, tiled=True)
    xcol_twin = near(lax.ppermute(xcol, "row", [(i, i ^ 1) for i in range(row_devs)]))
    turned = [
        near(lax.ppermute(pair, "col", [(i, i // runs * runs + (i + s) % runs) for i in range(col_devs)]))
        for s in range(1, runs)
    ]
    diag_term, stats = pl.pallas_call(
        diag_kernel,
        out_shape=(jax.ShapeDtypeStruct((width, span), F32), jax.ShapeDtypeStruct((2, width, LANES), F32)),
        in_specs=[VM, VM],
        out_specs=(VM, VM),
        compiler_params=params(4),
        cost_estimate=cost(1 << 28, 1 << 20),
    )(vectors, diag_blocks)
    diag_term, stats = near(diag_term), near(stats)
    x_row = near(pl.pallas_call(
        rows_kernel,
        out_shape=jax.ShapeDtypeStruct((col_devs * owned, width, LANES), BF16),
        in_specs=[VM] * (runs + 1) + [ANY],
        out_specs=VM,
        compiler_params=params(4),
        cost_estimate=cost(4 << 30, 8 << 20),
    )(vectors, beside, *turned, xcol))
    out_row, out_col = pl.pallas_call(
        block_kernel,
        out_shape=(
            jax.ShapeDtypeStruct((col_devs, width, span), BF16),
            jax.ShapeDtypeStruct((row_devs, width, wide), BF16),
        ),
        in_specs=[SM] * 3 + [VM] * 4 + [HBM],
        out_specs=(VM, VM),
        scratch_shapes=[
            pltpu.VMEM((row_devs * owned, width, LANES), BF16),
            pltpu.VMEM((col_devs * owned + 1, width, LANES), F32),
            pltpu.VMEM((row_devs * owned + 1, width, LANES), F32),
        ] + block_scratch,
        compiler_params=params(24),
    )(count, rows, cols, x_row, xcol, xcol_twin, stats, blocks)
    got_col = lax.all_to_all(out_col, "row", 0, 0, tiled=True)
    part, out_row = pl.pallas_call(
        middle_kernel,
        out_shape=(jax.ShapeDtypeStruct((width, span), F32), jax.ShapeDtypeStruct((col_devs, width, wide), BF16)),
        in_specs=[VM] * 3,
        out_specs=(VM, VM),
        compiler_params=params(8),
    )(got_col, diag_term, out_row)
    got_row = lax.all_to_all(out_row, "col", 0, 0, tiled=True)
    return pl.pallas_call(
        final_kernel,
        out_shape=(jax.ShapeDtypeStruct((width, span), F32), jax.ShapeDtypeStruct((width, span), BF16)),
        in_specs=[VM] * 4,
        out_specs=(VM, VM),
        compiler_params=params(8),
    )(got_row, part, vectors, precond)


def solution(mesh):
    placed = (
        P(None, ("row", "col")),
        P("row", "col", None, None, None),
        P("row", "col", None),
        P("row", "col", None),
        P("row", "col"),
        P(("row", "col"), None, None),
        P(("row", "col"), None, None),
    )
    return jax.shard_map(
        per_device,
        mesh=mesh,
        in_specs=placed,
        out_specs=(P(None, ("row", "col")), P(None, ("row", "col"))),
        check_vma=False,
    )
```

```python
import functools
import jax
import jax.numpy as jnp
from jax import lax
from jax.experimental import pallas as pl
from jax.experimental.pallas import tpu as pltpu
from jax.sharding import PartitionSpec as P

CHUNK = 16
GROUP = 8
LANES = 128
F32 = jnp.float32
BF16 = jnp.bfloat16


def split_tile(xy, xx, width):
    lane = lax.broadcasted_iota(jnp.int32, (width, LANES), 1)
    v = jnp.where(lane % 2 == 0, xy, xx)
    hi = v.astype(BF16).astype(F32)
    mid = (v - hi).astype(BF16).astype(F32)
    low = v - hi - mid
    tile = jnp.where(lane < 2, hi, jnp.where(lane < 4, mid, jnp.where(lane < 6, low, 0.0)))
    return tile.astype(BF16)


def join_tile(tile):
    lane = lax.broadcasted_iota(jnp.int32, tile.shape, 1)
    xy = jnp.sum(jnp.where(lane % 2 == 0, tile, 0.0), axis=1, keepdims=True)
    xx = jnp.sum(jnp.where(lane % 2 == 1, tile, 0.0), axis=1, keepdims=True)
    return xy, xx


def fetch(stiff_ref, buf, sems, count):
    copies = []
    for c in range(stiff_ref.shape[0] // CHUNK):
        here = pl.ds(c * CHUNK, CHUNK)
        copies.append(pltpu.make_async_copy(stiff_ref.at[here], buf.at[here], sems.at[c]))
    for c, copy in enumerate(copies):
        pl.when(c * CHUNK < count)(copy.start)
    return copies


def pair_products(xa, xb, blocks, turned):
    none = jnp.zeros_like(xa)
    x = jnp.concatenate([jnp.concatenate([xa, none], axis=1), jnp.concatenate([none, xb], axis=1)], axis=0)
    if turned:
        b = jnp.concatenate([blocks[0], blocks[1]], axis=1)
        dims = ((1,), (1,))
    else:
        b = blocks.reshape(2 * blocks.shape[1], blocks.shape[2])
        dims = ((1,), (0,))
    out = lax.dot_general(x, b, (dims, ((), ())), preferred_element_type=F32)
    return out[:xa.shape[0]], out[xa.shape[0]:]


def diag_kernel(x_ref, diag_ref, term_ref, stats_ref):
    width, span = x_ref.shape
    xy = jnp.zeros((width, LANES), F32)
    xx = jnp.zeros((width, LANES), F32)
    for g in range(span // LANES):
        here = slice(g * LANES, (g + 1) * LANES)
        xg = x_ref[:, here]
        d = diag_ref[g]
        term = lax.dot_general(xg, d, (((1,), (1,)), ((), ())), preferred_element_type=F32)
        term = term + lax.dot_general(xg, d, (((1,), (0,)), ((), ())), preferred_element_type=F32)
        term_ref[:, here] = term
        xf = xg.astype(F32)
        xy = xy + xf * term
        xx = xx + xf * xf
    stats_ref[0] = xy
    stats_ref[1] = xx


def rows_kernel(x_ref, z_ref, *refs):
    (*pair_refs, after_ref, x_row) = refs
    owned = x_ref.shape[1] // LANES
    runs = len(pair_refs) + 1
    place = lax.axis_index("col")
    zl = place // runs
    y = place % runs
    for s in range(runs):
        for k in range(2):
            dev = ((zl + k) % 2) * runs + (y + runs - s) % runs
            for t in range(owned):
                here = slice(t * LANES, (t + 1) * LANES)
                piece = (x_ref if k == 0 else z_ref)[:, here] if s == 0 else pair_refs[s - 1][k, :, here]
                x_row[dev * owned + t] = piece


def block_kernel(count_ref, rows_ref, cols_ref, x_row, xcol_ref, twin_ref, stats_ref, stiff_ref, *refs):
    (*ring_refs, row_keep, col_keep, core_out, x_col, acc_row, acc_col, buf, sems) = refs
    count = count_ref[0, 0]
    copies = fetch(stiff_ref, buf, sems, count)
    width, span = xcol_ref.shape[2:]
    owned = span // LANES
    acc_row[...] = jnp.zeros_like(acc_row)
    acc_col[...] = jnp.zeros_like(acc_col)
    place = lax.axis_index("row")
    high = (place // 2) % 2
    core = place % 2
    for line in range(xcol_ref.shape[0]):
        for k in range(2):
            for ref, twin in ((xcol_ref, 0), (twin_ref, 1)):
                dev = line * 4 + (high + k) % 2 * 2 + (core + twin) % 2
                for t in range(owned):
                    x_col[dev * owned + t] = ref[line, k, :, t * LANES:(t + 1) * LANES]
    for c, copy in enumerate(copies):

        @pl.when(c * CHUNK < count)
        def _():
            copy.wait()
            for h in range(0, CHUNK, GROUP):
                found = []
                for n in range(c * CHUNK + h, c * CHUNK + h + GROUP, 2):
                    i = [rows_ref[n + k] for k in range(2)]
                    j = [cols_ref[n + k] for k in range(2)]
                    to_row = pair_products(x_col[j[0]], x_col[j[1]], buf[n:n + 2], True)
                    to_col = pair_products(x_row[i[0]], x_row[i[1]], buf[n:n + 2], False)
                    for k in range(2):
                        live = n + k < count
                        found.append((acc_row, jnp.where(live, i[k], acc_row.shape[0] - 1), to_row[k]))
                        found.append((acc_col, jnp.where(live, j[k], acc_col.shape[0] - 1), to_col[k]))
                for acc, g, term in found:
                    acc[g] += term

    runs = len(ring_refs) + 1
    place = lax.axis_index("col")
    part = jnp.zeros((width, LANES), F32)
    for s in range(runs):
        for k in range(2):
            dev = (place // runs + k) % 2 * runs + (place + s) % runs
            for t in range(owned):
                here = slice(t * LANES, (t + 1) * LANES)
                a = acc_row[dev * owned + t]
                part = part + a * x_row[dev * owned + t].astype(F32)
                if s == 0:
                    row_keep[k, :, here] = a
                else:
                    ring_refs[s - 1][k, :, here] = a.astype(BF16)
    place = lax.axis_index("row")
    lines = xcol_ref.shape[0]
    for s in range(lines):
        for k in range(2):
            dev = (place // 4 + s) % lines * 4 + (place // 2 + k) % 2 * 2
            for t in range(owned):
                here = slice(t * LANES, (t + 1) * LANES)
                col_keep[2 * s + k, :, here] = acc_col[(dev + place % 2) * owned + t]
                core_out[2 * s + k, :, here] = acc_col[(dev + (place + 1) % 2) * owned + t].astype(BF16)
    xy = jnp.sum(2.0 * part + stats_ref[0], axis=1, keepdims=True)
    xx = jnp.sum(stats_ref[1], axis=1, keepdims=True)
    core_out[2 * lines, :, :LANES] = split_tile(xy, xx, width)
    core_out[2 * lines, :, LANES:] = jnp.zeros((width, span - LANES), BF16)


def tile_sum(first, *more):
    total = first.astype(F32)
    for tile in more:
        total = total + tile.astype(F32)
    return split_tile(*join_tile(total), first.shape[0])


def core_kernel(own_ref, got_ref, keep_ref, *refs):
    (*line_refs, col_keep, tile_ref) = refs
    span = own_ref.shape[2]
    last = keep_ref.shape[0]
    tile = tile_sum(own_ref[last, :, :LANES], got_ref[last, :, :LANES])
    tile_ref[...] = tile
    for n in range(keep_ref.shape[0]):
        s, k = divmod(n, 2)
        for t in range(span // LANES):
            here = slice(t * LANES, (t + 1) * LANES)
            total = keep_ref[n, :, here] + got_ref[n, :, here].astype(F32)
            if s == 0:
                col_keep[k, :, here] = total
            else:
                line_refs[s - 1][k, :, here] = total.astype(BF16)
        if s > 0:
            line_refs[s - 1][k, :, span:] = tile


def line_tile_kernel(tile_ref, *refs):
    *got, out = refs
    span = got[0].shape[2] - LANES
    out[...] = tile_sum(tile_ref[...], *[ref[0, :, span:] for ref in got])


def ring_tile_kernel(*refs):
    *tiles, col_raw, row_raw, col_out, row_out, out = refs
    span = col_raw.shape[1]
    tile = tile_sum(*[ref[...] for ref in tiles])
    out[...] = tile
    for raw, ref in ((col_raw, col_out), (row_raw, row_out)):
        ref[:, :span] = raw[...]
        ref[:, span:] = tile


def sums_kernel(diag_ref, col_keep, row_keep, *refs):
    (*got, own_ref, col_raw, row_raw) = refs
    half = len(got) // 2
    for t in range(own_ref.shape[1] // LANES):
        here = slice(t * LANES, (t + 1) * LANES)
        total = [[keep[k, :, here] for k in range(2)] for keep in (col_keep, row_keep)]
        for g, ref in enumerate(got):
            for k in range(2):
                total[g // half][k] = total[g // half][k] + ref[k, :, here].astype(F32)
        own_ref[:, here] = diag_ref[:, here] + total[0][0] + total[1][0]
        col_raw[:, here] = total[0][1].astype(BF16)
        row_raw[:, here] = total[1][1].astype(BF16)


def final_kernel(own_ref, col_ref, row_ref, tile_ref, across_ref, x_ref, pre_ref, image_ref, search_ref):
    span = own_ref.shape[1]
    tile = tile_ref[...].astype(F32) + across_ref[...].astype(F32)
    xy, xx = join_tile(tile + col_ref[:, span:].astype(F32) + row_ref[:, span:].astype(F32))
    theta = xy / xx
    for t in range(span // LANES):
        here = slice(t * LANES, (t + 1) * LANES)
        total = own_ref[:, here] + col_ref[:, here].astype(F32) + row_ref[:, here].astype(F32)
        image_ref[:, here] = total
        resid = (total - theta * x_ref[:, here].astype(F32)).astype(BF16)
        out = lax.dot_general(resid, pre_ref[t], (((1,), (1,)), ((), ())), preferred_element_type=F32)
        search_ref[:, here] = out.astype(BF16)


def prepare_kernel(x_ref, z_ref, h_ref, pair_ref, lines_ref):
    pair_ref[0] = x_ref[...]
    pair_ref[1] = z_ref[...]
    for d in range(lines_ref.shape[0]):
        lines_ref[d, 0] = x_ref[...]
        lines_ref[d, 1] = h_ref[...]


VM = pl.BlockSpec(memory_space=pltpu.VMEM)
SM = pl.BlockSpec(memory_space=pltpu.SMEM)
ANY = pl.BlockSpec(memory_space=pl.ANY)
HBM = pl.BlockSpec(memory_space=pltpu.HBM)


def near(x):
    return pltpu.with_memory_space_constraint(x, pltpu.VMEM)


def params(mib):
    return pltpu.CompilerParams(vmem_limit_bytes=mib << 20)


def cost(flops, moved):
    return pl.CostEstimate(flops=flops, bytes_accessed=moved, transcendentals=0)


def per_device(vectors, stiffness, block_row, block_col, block_count, diag_blocks, precond):
    width, span = vectors.shape
    owned, block_len, _ = diag_blocks.shape
    slots = stiffness.shape[2]
    row_devs = lax.axis_size("row")
    col_devs = lax.axis_size("col")
    runs = col_devs // 2
    wide = span + LANES
    count = block_count
    rows = block_row.reshape(slots)
    cols = block_col.reshape(slots)
    block_scratch = [pltpu.VMEM((slots, block_len, block_len), BF16), pltpu.SemaphoreType.DMA((slots // CHUNK,))]
    blocks = pltpu.with_memory_space_constraint(stiffness.reshape(slots, block_len, block_len), pltpu.HBM)

    beside = near(lax.ppermute(vectors, "col", [(i, (i + runs) % col_devs) for i in range(col_devs)]))
    above = near(lax.ppermute(vectors, "row", [(i, i ^ 2) for i in range(row_devs)]))
    lines = row_devs // 4
    pair, spread = pl.pallas_call(
        prepare_kernel,
        out_shape=(
            jax.ShapeDtypeStruct((2, width, span), BF16),
            jax.ShapeDtypeStruct((lines, 2, width, span), BF16),
        ),
        in_specs=[VM, VM, VM],
        out_specs=(VM, VM),
        compiler_params=params(4),
    )(vectors, beside, above)
    pair = near(pair)
    same_line = [[x * 4 + k for x in range(lines)] for k in range(4)]
    xcol = lax.all_to_all(spread, "row", 0, 0, axis_index_groups=same_line, tiled=True)
    xcol_twin = near(lax.ppermute(xcol, "row", [(i, i ^ 1) for i in range(row_devs)]))
    turned = [
        near(lax.ppermute(pair, "col", [(i, i // runs * runs + (i + s) % runs) for i in range(col_devs)]))
        for s in range(1, runs)
    ]
    diag_term, stats = pl.pallas_call(
        diag_kernel,
        out_shape=(jax.ShapeDtypeStruct((width, span), F32), jax.ShapeDtypeStruct((2, width, LANES), F32)),
        in_specs=[VM, VM],
        out_specs=(VM, VM),
        compiler_params=params(4),
        cost_estimate=cost(1 << 28, 1 << 20),
    )(vectors, diag_blocks)
    diag_term, stats = near(diag_term), near(stats)
    x_row = near(pl.pallas_call(
        rows_kernel,
        out_shape=jax.ShapeDtypeStruct((col_devs * owned, width, LANES), BF16),
        in_specs=[VM] * (runs + 1) + [ANY],
        out_specs=VM,
        compiler_params=params(4),
        cost_estimate=cost(4 << 30, 8 << 20),
    )(vectors, beside, *turned, xcol))
    def shape(*dims, dtype=BF16):
        return jax.ShapeDtypeStruct(dims, dtype)

    def along_y(x, s):
        return near(lax.ppermute(x, "col", [(i, i // runs * runs + (i + s) % runs) for i in range(col_devs)]))

    def along_x(x, s):
        return near(lax.ppermute(x, "row", [(i, (i + 4 * s) % row_devs) for i in range(row_devs)]))

    def call(kernel, out_shape, *args):
        return pl.pallas_call(
            kernel,
            out_shape=out_shape,
            in_specs=[VM] * len(args),
            out_specs=jax.tree.map(lambda _: VM, out_shape),
            compiler_params=params(4),
        )(*args)

    *ring, row_keep, col_keep, core_out = pl.pallas_call(
        block_kernel,
        out_shape=(
            *[shape(2, width, span)] * (runs - 1),
            shape(2, width, span, dtype=F32),
            shape(2 * lines, width, span, dtype=F32),
            shape(2 * lines + 1, width, span),
        ),
        in_specs=[SM] * 3 + [VM] * 4 + [HBM],
        out_specs=(VM,) * (runs + 2),
        scratch_shapes=[
            pltpu.VMEM((row_devs * owned, width, LANES), BF16),
            pltpu.VMEM((col_devs * owned + 1, width, LANES), F32),
            pltpu.VMEM((row_devs * owned + 1, width, LANES), F32),
        ] + block_scratch,
        compiler_params=params(24),
    )(count, rows, cols, x_row, xcol, xcol_twin, stats, blocks)
    got_core = near(lax.ppermute(core_out, "row", [(i, i ^ 1) for i in range(row_devs)]))
    *line, col_keep, tile = call(
        core_kernel,
        (*[shape(2, width, wide)] * (lines - 1), shape(2, width, span, dtype=F32), shape(width, LANES)),
        core_out, got_core, col_keep,
    )
    line = [along_x(part, s + 1) for s, part in enumerate(line)]
    ring = [along_y(part, s + 1) for s, part in enumerate(ring)]
    tile = call(line_tile_kernel, shape(width, LANES), tile, *line)
    tiles = [along_y(tile, s) for s in range(1, runs)]
    own, col_raw, row_raw = call(
        sums_kernel,
        (shape(width, span, dtype=F32), shape(width, span), shape(width, span)),
        diag_term, col_keep, row_keep, *line, *ring,
    )
    col_out, row_out, tile = call(
        ring_tile_kernel,
        (shape(width, wide), shape(width, wide), shape(width, LANES)),
        tile, *tiles, col_raw, row_raw,
    )
    got_col = near(lax.ppermute(col_out, "row", [(i, i ^ 2) for i in range(row_devs)]))
    got_row = near(lax.ppermute(row_out, "col", [(i, (i + runs) % col_devs) for i in range(col_devs)]))
    across = near(lax.ppermute(
        tile, ("row", "col"),
        [(r * col_devs + c, (r ^ 2) * col_devs + (c + runs) % col_devs) for r in range(row_devs) for c in range(col_devs)],
    ))
    return pl.pallas_call(
        final_kernel,
        out_shape=(shape(width, span, dtype=F32), shape(width, span)),
        in_specs=[VM] * 7,
        out_specs=(VM, VM),
        compiler_params=params(4),
    )(own, got_col, got_row, tile, across, vectors, precond)


def solution(mesh):
    placed = (
        P(None, ("row", "col")),
        P("row", "col", None, None, None),
        P("row", "col", None),
        P("row", "col", None),
        P("row", "col"),
        P(("row", "col"), None, None),
        P(("row", "col"), None, None),
    )
    return jax.shard_map(
        per_device,
        mesh=mesh,
        in_specs=placed,
        out_specs=(P(None, ("row", "col")), P(None, ("row", "col"))),
        check_vma=False,
    )
```

```python
import functools
import jax
import jax.numpy as jnp
from jax import lax
from jax.experimental import pallas as pl
from jax.experimental.pallas import tpu as pltpu
from jax.sharding import PartitionSpec as P

CHUNK = 16
GROUP = 8
LANES = 128
F32 = jnp.float32
BF16 = jnp.bfloat16


def split_tile(xy, xx, width):
    lane = lax.broadcasted_iota(jnp.int32, (width, LANES), 1)
    v = jnp.where(lane % 2 == 0, xy, xx)
    hi = v.astype(BF16).astype(F32)
    mid = (v - hi).astype(BF16).astype(F32)
    low = v - hi - mid
    tile = jnp.where(lane < 2, hi, jnp.where(lane < 4, mid, jnp.where(lane < 6, low, 0.0)))
    return tile.astype(BF16)


def join_tile(tile):
    lane = lax.broadcasted_iota(jnp.int32, tile.shape, 1)
    xy = jnp.sum(jnp.where(lane % 2 == 0, tile, 0.0), axis=1, keepdims=True)
    xx = jnp.sum(jnp.where(lane % 2 == 1, tile, 0.0), axis=1, keepdims=True)
    return xy, xx


def fetch(stiff_ref, buf, sems, count):
    copies = []
    for c in range(stiff_ref.shape[0] // CHUNK):
        here = pl.ds(c * CHUNK, CHUNK)
        copies.append(pltpu.make_async_copy(stiff_ref.at[here], buf.at[here], sems.at[c]))
    for c, copy in enumerate(copies):
        pl.when(c * CHUNK < count)(copy.start)
    return copies


def pair_products(xa, xb, blocks, turned):
    none = jnp.zeros_like(xa)
    x = jnp.concatenate([jnp.concatenate([xa, none], axis=1), jnp.concatenate([none, xb], axis=1)], axis=0)
    if turned:
        b = jnp.concatenate([blocks[0], blocks[1]], axis=1)
        dims = ((1,), (1,))
    else:
        b = blocks.reshape(2 * blocks.shape[1], blocks.shape[2])
        dims = ((1,), (0,))
    out = lax.dot_general(x, b, (dims, ((), ())), preferred_element_type=F32)
    return out[:xa.shape[0]], out[xa.shape[0]:]


def diag_kernel(x_ref, diag_ref, term_ref, stats_ref, near_ref):
    width, span = x_ref.shape
    xy = jnp.zeros((width, LANES), F32)
    xx = jnp.zeros((width, LANES), F32)
    for g in range(span // LANES):
        here = slice(g * LANES, (g + 1) * LANES)
        xg = x_ref[:, here]
        d = diag_ref[g]
        term = lax.dot_general(xg, d, (((1,), (1,)), ((), ())), preferred_element_type=F32)
        term = term + lax.dot_general(xg, d, (((1,), (0,)), ((), ())), preferred_element_type=F32)
        term_ref[:, here] = term
        xf = xg.astype(F32)
        xy = xy + xf * term
        xx = xx + xf * xf
    stats_ref[0] = xy
    stats_ref[1] = xx
    near_ref[...] = x_ref[...]


def rows_kernel(x_ref, z_ref, *refs):
    (*pair_refs, after_ref, x_row) = refs
    owned = x_ref.shape[1] // LANES
    runs = len(pair_refs) + 1
    place = lax.axis_index("col")
    zl = place // runs
    y = place % runs
    for s in range(runs):
        for k in range(2):
            dev = ((zl + k) % 2) * runs + (y + runs - s) % runs
            for t in range(owned):
                here = slice(t * LANES, (t + 1) * LANES)
                piece = (x_ref if k == 0 else z_ref)[:, here] if s == 0 else pair_refs[s - 1][k, :, here]
                x_row[dev * owned + t] = piece


def block_kernel(count_ref, rows_hbm, cols_hbm, x_row, xcol_ref, twin_ref, stats_ref, stiff_ref, *refs):
    (*ring_refs, row_keep, col_keep, core_out, x_col, acc_row, acc_col, buf, rows_ref, cols_ref, sems, index_sems) = refs
    count = count_ref[0, 0]
    index_copies = [
        pltpu.make_async_copy(rows_hbm, rows_ref, index_sems.at[0]),
        pltpu.make_async_copy(cols_hbm, cols_ref, index_sems.at[1]),
    ]
    for copy in index_copies:
        copy.start()
    copies = fetch(stiff_ref, buf, sems, count)
    width, span = xcol_ref.shape[2:]
    owned = span // LANES
    acc_row[...] = jnp.zeros_like(acc_row)
    acc_col[...] = jnp.zeros_like(acc_col)
    place = lax.axis_index("row")
    high = (place // 2) % 2
    core = place % 2
    for line in range(xcol_ref.shape[0]):
        for k in range(2):
            for ref, twin in ((xcol_ref, 0), (twin_ref, 1)):
                dev = line * 4 + (high + k) % 2 * 2 + (core + twin) % 2
                for t in range(owned):
                    x_col[dev * owned + t] = ref[line, k, :, t * LANES:(t + 1) * LANES]
    for copy in index_copies:
        copy.wait()
    for c, copy in enumerate(copies):

        @pl.when(c * CHUNK < count)
        def _():
            copy.wait()
            for h in range(0, CHUNK, GROUP):
                found = []
                for n in range(c * CHUNK + h, c * CHUNK + h + GROUP, 2):
                    i = [rows_ref[n + k] for k in range(2)]
                    j = [cols_ref[n + k] for k in range(2)]
                    to_row = pair_products(x_col[j[0]], x_col[j[1]], buf[n:n + 2], True)
                    to_col = pair_products(x_row[i[0]], x_row[i[1]], buf[n:n + 2], False)
                    for k in range(2):
                        live = n + k < count
                        found.append((acc_row, jnp.where(live, i[k], acc_row.shape[0] - 1), to_row[k]))
                        found.append((acc_col, jnp.where(live, j[k], acc_col.shape[0] - 1), to_col[k]))
                for acc, g, term in found:
                    acc[g] += term

    runs = len(ring_refs) + 1
    place = lax.axis_index("col")
    part = jnp.zeros((width, LANES), F32)
    for s in range(runs):
        for k in range(2):
            dev = (place // runs + k) % 2 * runs + (place + s) % runs
            for t in range(owned):
                here = slice(t * LANES, (t + 1) * LANES)
                a = acc_row[dev * owned + t]
                part = part + a * x_row[dev * owned + t].astype(F32)
                if s == 0:
                    row_keep[k, :, here] = a
                else:
                    ring_refs[s - 1][k, :, here] = a.astype(BF16)
    place = lax.axis_index("row")
    lines = xcol_ref.shape[0]
    for s in range(lines):
        for k in range(2):
            dev = (place // 4 + s) % lines * 4 + (place // 2 + k) % 2 * 2
            for t in range(owned):
                here = slice(t * LANES, (t + 1) * LANES)
                col_keep[2 * s + k, :, here] = acc_col[(dev + place % 2) * owned + t]
                core_out[2 * s + k, :, here] = acc_col[(dev + (place + 1) % 2) * owned + t].astype(BF16)
    xy = jnp.sum(2.0 * part + stats_ref[0], axis=1, keepdims=True)
    xx = jnp.sum(stats_ref[1], axis=1, keepdims=True)
    core_out[2 * lines, :, :LANES] = split_tile(xy, xx, width)
    core_out[2 * lines, :, LANES:] = jnp.zeros((width, span - LANES), BF16)


def tile_sum(first, *more):
    total = first.astype(F32)
    for tile in more:
        total = total + tile.astype(F32)
    return split_tile(*join_tile(total), first.shape[0])


def core_kernel(own_ref, got_ref, keep_ref, *refs):
    (*line_refs, col_keep, tile_ref) = refs
    span = own_ref.shape[2]
    last = keep_ref.shape[0]
    tile = tile_sum(own_ref[last, :, :LANES], got_ref[last, :, :LANES])
    tile_ref[...] = tile
    for n in range(keep_ref.shape[0]):
        s, k = divmod(n, 2)
        for t in range(span // LANES):
            here = slice(t * LANES, (t + 1) * LANES)
            total = keep_ref[n, :, here] + got_ref[n, :, here].astype(F32)
            if s == 0:
                col_keep[k, :, here] = total
            else:
                line_refs[s - 1][k, :, here] = total.astype(BF16)
        if s > 0:
            line_refs[s - 1][k, :, span:] = tile


def line_tile_kernel(tile_ref, *refs):
    *got, out = refs
    span = got[0].shape[2] - LANES
    out[...] = tile_sum(tile_ref[...], *[ref[0, :, span:] for ref in got])


def ring_tile_kernel(*refs):
    *tiles, col_raw, row_raw, col_out, row_out, out = refs
    span = col_raw.shape[1]
    tile = tile_sum(*[ref[...] for ref in tiles])
    out[...] = tile
    for raw, ref in ((col_raw, col_out), (row_raw, row_out)):
        ref[:, :span] = raw[...]
        ref[:, span:] = tile


def sums_kernel(diag_ref, col_keep, row_keep, *refs):
    (*got, own_ref, col_raw, row_raw) = refs
    half = len(got) // 2
    for t in range(own_ref.shape[1] // LANES):
        here = slice(t * LANES, (t + 1) * LANES)
        total = [[keep[k, :, here] for k in range(2)] for keep in (col_keep, row_keep)]
        for g, ref in enumerate(got):
            for k in range(2):
                total[g // half][k] = total[g // half][k] + ref[k, :, here].astype(F32)
        own_ref[:, here] = diag_ref[:, here] + total[0][0] + total[1][0]
        col_raw[:, here] = total[0][1].astype(BF16)
        row_raw[:, here] = total[1][1].astype(BF16)


def final_kernel(own_ref, col_ref, row_ref, tile_ref, across_ref, x_ref, pre_ref, image_ref, search_ref):
    span = own_ref.shape[1]
    tile = tile_ref[...].astype(F32) + across_ref[...].astype(F32)
    xy, xx = join_tile(tile + col_ref[:, span:].astype(F32) + row_ref[:, span:].astype(F32))
    theta = xy / xx
    for t in range(span // LANES):
        here = slice(t * LANES, (t + 1) * LANES)
        total = own_ref[:, here] + col_ref[:, here].astype(F32) + row_ref[:, here].astype(F32)
        image_ref[:, here] = total
        resid = (total - theta * x_ref[:, here].astype(F32)).astype(BF16)
        out = lax.dot_general(resid, pre_ref[t], (((1,), (1,)), ((), ())), preferred_element_type=F32)
        search_ref[:, here] = out.astype(BF16)


def prepare_kernel(x_ref, z_ref, h_ref, pair_ref, lines_ref):
    pair_ref[0] = x_ref[...]
    pair_ref[1] = z_ref[...]
    for d in range(lines_ref.shape[0]):
        lines_ref[d, 0] = x_ref[...]
        lines_ref[d, 1] = h_ref[...]


VM = pl.BlockSpec(memory_space=pltpu.VMEM)
SM = pl.BlockSpec(memory_space=pltpu.SMEM)
ANY = pl.BlockSpec(memory_space=pl.ANY)
HBM = pl.BlockSpec(memory_space=pltpu.HBM)


def near(x):
    return pltpu.with_memory_space_constraint(x, pltpu.VMEM)


def params(mib):
    return pltpu.CompilerParams(vmem_limit_bytes=mib << 20)


def cost(flops, moved):
    return pl.CostEstimate(flops=flops, bytes_accessed=moved, transcendentals=0)


def per_device(vectors, stiffness, block_row, block_col, block_count, diag_blocks, precond):
    width, span = vectors.shape
    owned, block_len, _ = diag_blocks.shape
    slots = stiffness.shape[2]
    row_devs = lax.axis_size("row")
    col_devs = lax.axis_size("col")
    runs = col_devs // 2
    wide = span + LANES
    count = block_count
    rows = pltpu.with_memory_space_constraint(block_row.reshape(slots), pltpu.HBM)
    cols = pltpu.with_memory_space_constraint(block_col.reshape(slots), pltpu.HBM)
    block_scratch = [
        pltpu.VMEM((slots, block_len, block_len), BF16),
        pltpu.SMEM((slots,), jnp.int32),
        pltpu.SMEM((slots,), jnp.int32),
        pltpu.SemaphoreType.DMA((slots // CHUNK,)),
        pltpu.SemaphoreType.DMA((2,)),
    ]
    blocks = pltpu.with_memory_space_constraint(stiffness.reshape(slots, block_len, block_len), pltpu.HBM)

    beside = near(lax.ppermute(vectors, "col", [(i, (i + runs) % col_devs) for i in range(col_devs)]))
    across_z = [
        (r * col_devs + c, (r ^ 2) * col_devs + (c + runs) % col_devs)
        for r in range(row_devs)
        for c in range(col_devs)
    ]
    above = near(lax.ppermute(vectors, "row", [(i, i ^ 2) for i in range(row_devs)]))
    diag_term, stats, own_x = pl.pallas_call(
        diag_kernel,
        out_shape=(
            jax.ShapeDtypeStruct((width, span), F32),
            jax.ShapeDtypeStruct((2, width, LANES), F32),
            jax.ShapeDtypeStruct((width, span), BF16),
        ),
        in_specs=[VM, VM],
        out_specs=(VM, VM, VM),
        compiler_params=params(4),
        cost_estimate=cost(1 << 30, 4 << 20),
    )(vectors, diag_blocks)
    diag_term, stats, own_x = near(diag_term), near(stats), near(own_x)
    lines = row_devs // 4
    pair, spread = pl.pallas_call(
        prepare_kernel,
        out_shape=(
            jax.ShapeDtypeStruct((2, width, span), BF16),
            jax.ShapeDtypeStruct((lines, 2, width, span), BF16),
        ),
        in_specs=[VM, VM, VM],
        out_specs=(VM, VM),
        compiler_params=params(4),
    )(own_x, beside, above)
    pair = near(pair)
    same_line = [[x * 4 + k for x in range(lines)] for k in range(4)]
    xcol = lax.all_to_all(spread, "row", 0, 0, axis_index_groups=same_line, tiled=True)
    xcol_twin = near(lax.ppermute(xcol, "row", [(i, i ^ 1) for i in range(row_devs)]))
    turned = [
        near(lax.ppermute(pair, "col", [(i, i // runs * runs + (i + s) % runs) for i in range(col_devs)]))
        for s in range(1, runs)
    ]
    x_row = near(pl.pallas_call(
        rows_kernel,
        out_shape=jax.ShapeDtypeStruct((col_devs * owned, width, LANES), BF16),
        in_specs=[VM] * (runs + 1) + [ANY],
        out_specs=VM,
        compiler_params=params(4),
        cost_estimate=cost(4 << 30, 8 << 20),
    )(own_x, beside, *turned, xcol))
    def shape(*dims, dtype=BF16):
        return jax.ShapeDtypeStruct(dims, dtype)

    def along_y(x, s):
        return near(lax.ppermute(x, "col", [(i, i // runs * runs + (i + s) % runs) for i in range(col_devs)]))

    def along_x(x, s):
        return near(lax.ppermute(x, "row", [(i, (i + 4 * s) % row_devs) for i in range(row_devs)]))

    def call(kernel, out_shape, *args):
        return pl.pallas_call(
            kernel,
            out_shape=out_shape,
            in_specs=[VM] * len(args),
            out_specs=jax.tree.map(lambda _: VM, out_shape),
            compiler_params=params(4),
        )(*args)

    *ring, row_keep, col_keep, core_out = pl.pallas_call(
        block_kernel,
        out_shape=(
            *[shape(2, width, span)] * (runs - 1),
            shape(2, width, span, dtype=F32),
            shape(2 * lines, width, span, dtype=F32),
            shape(2 * lines + 1, width, span),
        ),
        in_specs=[SM, HBM, HBM] + [VM] * 4 + [HBM],
        out_specs=(VM,) * (runs + 2),
        scratch_shapes=[
            pltpu.VMEM((row_devs * owned, width, LANES), BF16),
            pltpu.VMEM((col_devs * owned + 1, width, LANES), F32),
            pltpu.VMEM((row_devs * owned + 1, width, LANES), F32),
        ] + block_scratch,
        compiler_params=params(24),
    )(count, rows, cols, x_row, xcol, xcol_twin, stats, blocks)
    got_core = near(lax.ppermute(core_out, "row", [(i, i ^ 1) for i in range(row_devs)]))
    *line, col_keep, tile = call(
        core_kernel,
        (*[shape(2, width, wide)] * (lines - 1), shape(2, width, span, dtype=F32), shape(width, LANES)),
        core_out, got_core, col_keep,
    )
    line = [along_x(part, s + 1) for s, part in enumerate(line)]
    ring = [along_y(part, s + 1) for s, part in enumerate(ring)]
    tile = call(line_tile_kernel, shape(width, LANES), tile, *line)
    tiles = [along_y(tile, s) for s in range(1, runs)]
    own, col_raw, row_raw = call(
        sums_kernel,
        (shape(width, span, dtype=F32), shape(width, span), shape(width, span)),
        diag_term, col_keep, row_keep, *line, *ring,
    )
    col_out, row_out, tile = call(
        ring_tile_kernel,
        (shape(width, wide), shape(width, wide), shape(width, LANES)),
        tile, *tiles, col_raw, row_raw,
    )
    got_col = near(lax.ppermute(col_out, "row", [(i, i ^ 2) for i in range(row_devs)]))
    got_row = near(lax.ppermute(row_out, "col", [(i, (i + runs) % col_devs) for i in range(col_devs)]))
    across = near(lax.ppermute(tile, ("row", "col"), across_z))
    return pl.pallas_call(
        final_kernel,
        out_shape=(shape(width, span, dtype=F32), shape(width, span)),
        in_specs=[VM] * 7,
        out_specs=(VM, VM),
        compiler_params=params(4),
    )(own, got_col, got_row, tile, across, own_x, precond)


def solution(mesh):
    placed = (
        P(None, ("row", "col")),
        P("row", "col", None, None, None),
        P("row", "col", None),
        P("row", "col", None),
        P("row", "col"),
        P(("row", "col"), None, None),
        P(("row", "col"), None, None),
    )
    return jax.shard_map(
        per_device,
        mesh=mesh,
        in_specs=placed,
        out_specs=(P(None, ("row", "col")), P(None, ("row", "col"))),
        check_vma=False,
    )
```

```python
import functools
import jax
import jax.numpy as jnp
from jax import lax
from jax.experimental import pallas as pl
from jax.experimental.pallas import tpu as pltpu
from jax.sharding import PartitionSpec as P

CHUNK = 32
GROUP = 8
LANES = 128
F32 = jnp.float32
BF16 = jnp.bfloat16


def split_tile(xy, xx, width):
    lane = lax.broadcasted_iota(jnp.int32, (width, LANES), 1)
    v = jnp.where(lane % 2 == 0, xy, xx)
    hi = v.astype(BF16).astype(F32)
    mid = (v - hi).astype(BF16).astype(F32)
    low = v - hi - mid
    tile = jnp.where(lane < 2, hi, jnp.where(lane < 4, mid, jnp.where(lane < 6, low, 0.0)))
    return tile.astype(BF16)


def join_tile(tile):
    lane = lax.broadcasted_iota(jnp.int32, tile.shape, 1)
    xy = jnp.sum(jnp.where(lane % 2 == 0, tile, 0.0), axis=1, keepdims=True)
    xx = jnp.sum(jnp.where(lane % 2 == 1, tile, 0.0), axis=1, keepdims=True)
    return xy, xx


def fetch(stiff_ref, buf, sems, count):
    copies = []
    for c in range(stiff_ref.shape[0] // CHUNK):
        here = pl.ds(c * CHUNK, CHUNK)
        copies.append(pltpu.make_async_copy(stiff_ref.at[here], buf.at[here], sems.at[c]))
    for c, copy in enumerate(copies):
        pl.when(c * CHUNK < count)(copy.start)
    return copies


def pair_products(xa, xb, blocks, turned):
    none = jnp.zeros_like(xa)
    x = jnp.concatenate([jnp.concatenate([xa, none], axis=1), jnp.concatenate([none, xb], axis=1)], axis=0)
    if turned:
        b = jnp.concatenate([blocks[0], blocks[1]], axis=1)
        dims = ((1,), (1,))
    else:
        b = blocks.reshape(2 * blocks.shape[1], blocks.shape[2])
        dims = ((1,), (0,))
    out = lax.dot_general(x, b, (dims, ((), ())), preferred_element_type=F32)
    return out[:xa.shape[0]], out[xa.shape[0]:]


def diag_kernel(x_ref, diag_ref, term_ref, stats_ref, near_ref):
    width, span = x_ref.shape
    xy = jnp.zeros((width, LANES), F32)
    xx = jnp.zeros((width, LANES), F32)
    for g in range(span // LANES):
        here = slice(g * LANES, (g + 1) * LANES)
        xg = x_ref[:, here]
        d = diag_ref[g]
        term = lax.dot_general(xg, d, (((1,), (1,)), ((), ())), preferred_element_type=F32)
        term = term + lax.dot_general(xg, d, (((1,), (0,)), ((), ())), preferred_element_type=F32)
        term_ref[:, here] = term
        xf = xg.astype(F32)
        xy = xy + xf * term
        xx = xx + xf * xf
    stats_ref[0] = xy
    stats_ref[1] = xx
    near_ref[...] = x_ref[...]


def rows_kernel(x_ref, z_ref, *refs):
    (*pair_refs, after_ref, x_row) = refs
    owned = x_ref.shape[1] // LANES
    runs = len(pair_refs) + 1
    place = lax.axis_index("col")
    zl = place // runs
    y = place % runs
    for s in range(runs):
        for k in range(2):
            dev = ((zl + k) % 2) * runs + (y + runs - s) % runs
            for t in range(owned):
                here = slice(t * LANES, (t + 1) * LANES)
                piece = (x_ref if k == 0 else z_ref)[:, here] if s == 0 else pair_refs[s - 1][k, :, here]
                x_row[dev * owned + t] = piece


def block_kernel(count_ref, rows_hbm, cols_hbm, x_row, xcol_ref, twin_ref, stats_ref, stiff_ref, *refs):
    (*ring_refs, row_keep, col_keep, core_out, x_col, acc_row, acc_col, buf, rows_ref, cols_ref, sems, index_sems) = refs
    count = count_ref[0, 0]
    index_copies = [
        pltpu.make_async_copy(rows_hbm, rows_ref, index_sems.at[0]),
        pltpu.make_async_copy(cols_hbm, cols_ref, index_sems.at[1]),
    ]
    for copy in index_copies:
        copy.start()
    copies = fetch(stiff_ref, buf, sems, count)
    width, span = xcol_ref.shape[2:]
    owned = span // LANES
    acc_row[...] = jnp.zeros_like(acc_row)
    acc_col[...] = jnp.zeros_like(acc_col)
    place = lax.axis_index("row")
    lines = xcol_ref.shape[0]
    for s in range(lines):
        for k in range(2):
            for twin, ref in enumerate((xcol_ref, twin_ref)):
                dev = (place // 4 + lines - s) % lines * 4 + (place // 2 + k) % 2 * 2 + (place + twin) % 2
                for t in range(owned):
                    x_col[dev * owned + t] = ref[s, k, :, t * LANES:(t + 1) * LANES]
    for copy in index_copies:
        copy.wait()
    for c, copy in enumerate(copies):

        @pl.when(c * CHUNK < count)
        def _():
            copy.wait()
            for h in range(0, CHUNK, GROUP):
                found = []
                for n in range(c * CHUNK + h, c * CHUNK + h + GROUP, 2):
                    i = [rows_ref[n + k] for k in range(2)]
                    j = [cols_ref[n + k] for k in range(2)]
                    to_row = pair_products(x_col[j[0]], x_col[j[1]], buf[n:n + 2], True)
                    to_col = pair_products(x_row[i[0]], x_row[i[1]], buf[n:n + 2], False)
                    for k in range(2):
                        live = n + k < count
                        found.append((acc_row, jnp.where(live, i[k], acc_row.shape[0] - 1), to_row[k]))
                        found.append((acc_col, jnp.where(live, j[k], acc_col.shape[0] - 1), to_col[k]))
                for acc, g, term in found:
                    acc[g] += term

    runs = len(ring_refs) + 1
    place = lax.axis_index("col")
    part = jnp.zeros((width, LANES), F32)
    for s in range(runs):
        for k in range(2):
            dev = (place // runs + k) % 2 * runs + (place + s) % runs
            for t in range(owned):
                here = slice(t * LANES, (t + 1) * LANES)
                a = acc_row[dev * owned + t]
                part = part + a * x_row[dev * owned + t].astype(F32)
                if s == 0:
                    row_keep[k, :, here] = a
                else:
                    ring_refs[s - 1][k, :, here] = a.astype(BF16)
    place = lax.axis_index("row")
    lines = xcol_ref.shape[0]
    for s in range(lines):
        for k in range(2):
            dev = (place // 4 + s) % lines * 4 + (place // 2 + k) % 2 * 2
            for t in range(owned):
                here = slice(t * LANES, (t + 1) * LANES)
                col_keep[2 * s + k, :, here] = acc_col[(dev + place % 2) * owned + t]
                core_out[2 * s + k, :, here] = acc_col[(dev + (place + 1) % 2) * owned + t].astype(BF16)
    xy = jnp.sum(2.0 * part + stats_ref[0], axis=1, keepdims=True)
    xx = jnp.sum(stats_ref[1], axis=1, keepdims=True)
    core_out[2 * lines, :, :LANES] = split_tile(xy, xx, width)
    core_out[2 * lines, :, LANES:] = jnp.zeros((width, span - LANES), BF16)


def tile_sum(first, *more):
    total = first.astype(F32)
    for tile in more:
        total = total + tile.astype(F32)
    return split_tile(*join_tile(total), first.shape[0])


def core_kernel(own_ref, got_ref, keep_ref, *refs):
    (*line_refs, col_keep, tile_ref) = refs
    span = own_ref.shape[2]
    last = keep_ref.shape[0]
    tile = tile_sum(own_ref[last, :, :LANES], got_ref[last, :, :LANES])
    tile_ref[...] = tile
    for n in range(keep_ref.shape[0]):
        s, k = divmod(n, 2)
        for t in range(span // LANES):
            here = slice(t * LANES, (t + 1) * LANES)
            total = keep_ref[n, :, here] + got_ref[n, :, here].astype(F32)
            if s == 0:
                col_keep[k, :, here] = total
            else:
                line_refs[s - 1][k, :, here] = total.astype(BF16)
        if s > 0:
            line_refs[s - 1][k, :, span:] = tile


def line_tile_kernel(tile_ref, *refs):
    *got, out = refs
    span = got[0].shape[2] - LANES
    out[...] = tile_sum(tile_ref[...], *[ref[0, :, span:] for ref in got])


def ring_tile_kernel(*refs):
    *tiles, col_raw, row_raw, col_out, row_out, out = refs
    span = col_raw.shape[1]
    tile = tile_sum(*[ref[...] for ref in tiles])
    out[...] = tile
    for raw, ref in ((col_raw, col_out), (row_raw, row_out)):
        ref[:, :span] = raw[...]
        ref[:, span:] = tile


def sums_kernel(diag_ref, col_keep, row_keep, *refs):
    (*got, own_ref, col_raw, row_raw) = refs
    half = len(got) // 2
    for t in range(own_ref.shape[1] // LANES):
        here = slice(t * LANES, (t + 1) * LANES)
        total = [[keep[k, :, here] for k in range(2)] for keep in (col_keep, row_keep)]
        for g, ref in enumerate(got):
            for k in range(2):
                total[g // half][k] = total[g // half][k] + ref[k, :, here].astype(F32)
        own_ref[:, here] = diag_ref[:, here] + total[0][0] + total[1][0]
        col_raw[:, here] = total[0][1].astype(BF16)
        row_raw[:, here] = total[1][1].astype(BF16)


def final_kernel(own_ref, col_ref, row_ref, tile_ref, across_ref, x_ref, pre_ref, image_ref, search_ref):
    span = own_ref.shape[1]
    tile = tile_ref[...].astype(F32) + across_ref[...].astype(F32)
    xy, xx = join_tile(tile + col_ref[:, span:].astype(F32) + row_ref[:, span:].astype(F32))
    theta = xy / xx
    for t in range(span // LANES):
        here = slice(t * LANES, (t + 1) * LANES)
        total = own_ref[:, here] + col_ref[:, here].astype(F32) + row_ref[:, here].astype(F32)
        image_ref[:, here] = total
        resid = (total - theta * x_ref[:, here].astype(F32)).astype(BF16)
        out = lax.dot_general(resid, pre_ref[t], (((1,), (1,)), ((), ())), preferred_element_type=F32)
        search_ref[:, here] = out.astype(BF16)


def pairs_kernel(x_ref, z_ref, h_ref, ring_ref, line_ref):
    for ref, other in ((ring_ref, z_ref), (line_ref, h_ref)):
        ref[0] = x_ref[...]
        ref[1] = other[...]


def stack_kernel(*refs):
    *parts, out = refs
    for s, ref in enumerate(parts):
        out[s] = ref[...]


VM = pl.BlockSpec(memory_space=pltpu.VMEM)
SM = pl.BlockSpec(memory_space=pltpu.SMEM)
ANY = pl.BlockSpec(memory_space=pl.ANY)
HBM = pl.BlockSpec(memory_space=pltpu.HBM)


def near(x):
    return pltpu.with_memory_space_constraint(x, pltpu.VMEM)


def params(mib):
    return pltpu.CompilerParams(vmem_limit_bytes=mib << 20)


def cost(flops, moved):
    return pl.CostEstimate(flops=flops, bytes_accessed=moved, transcendentals=0)


def per_device(vectors, stiffness, block_row, block_col, block_count, diag_blocks, precond):
    width, span = vectors.shape
    owned, block_len, _ = diag_blocks.shape
    slots = stiffness.shape[2]
    row_devs = lax.axis_size("row")
    col_devs = lax.axis_size("col")
    runs = col_devs // 2
    wide = span + LANES
    count = block_count
    rows = pltpu.with_memory_space_constraint(block_row.reshape(slots), pltpu.HBM)
    cols = pltpu.with_memory_space_constraint(block_col.reshape(slots), pltpu.HBM)
    block_scratch = [
        pltpu.VMEM((slots, block_len, block_len), BF16),
        pltpu.SMEM((slots,), jnp.int32),
        pltpu.SMEM((slots,), jnp.int32),
        pltpu.SemaphoreType.DMA((slots // CHUNK,)),
        pltpu.SemaphoreType.DMA((2,)),
    ]
    blocks = pltpu.with_memory_space_constraint(stiffness.reshape(slots, block_len, block_len), pltpu.HBM)

    beside = near(lax.ppermute(vectors, "col", [(i, (i + runs) % col_devs) for i in range(col_devs)]))
    across_z = [
        (r * col_devs + c, (r ^ 2) * col_devs + (c + runs) % col_devs)
        for r in range(row_devs)
        for c in range(col_devs)
    ]
    above = near(lax.ppermute(vectors, "row", [(i, i ^ 2) for i in range(row_devs)]))
    diag_term, stats, own_x = pl.pallas_call(
        diag_kernel,
        out_shape=(
            jax.ShapeDtypeStruct((width, span), F32),
            jax.ShapeDtypeStruct((2, width, LANES), F32),
            jax.ShapeDtypeStruct((width, span), BF16),
        ),
        in_specs=[VM, VM],
        out_specs=(VM, VM, VM),
        compiler_params=params(4),
        cost_estimate=cost(1 << 30, 4 << 20),
    )(vectors, diag_blocks)
    diag_term, stats, own_x = near(diag_term), near(stats), near(own_x)
    lines = row_devs // 4
    pair, line = pl.pallas_call(
        pairs_kernel,
        out_shape=(jax.ShapeDtypeStruct((2, width, span), BF16),) * 2,
        in_specs=[VM, VM, VM],
        out_specs=(VM, VM),
        compiler_params=params(4),
    )(own_x, beside, above)
    pair, line = near(pair), near(line)
    passed = [
        near(lax.ppermute(line, "row", [(i, (i + 4 * s) % row_devs) for i in range(row_devs)])) for s in range(1, lines)
    ]
    xcol = near(pl.pallas_call(
        stack_kernel,
        out_shape=jax.ShapeDtypeStruct((lines, 2, width, span), BF16),
        in_specs=[VM] * lines,
        out_specs=VM,
        compiler_params=params(4),
        cost_estimate=cost(0, 1 << 20),
    )(line, *passed))
    xcol_twin = near(lax.ppermute(xcol, "row", [(i, i ^ 1) for i in range(row_devs)]))
    turned = [
        near(lax.ppermute(pair, "col", [(i, i // runs * runs + (i + s) % runs) for i in range(col_devs)]))
        for s in range(1, runs)
    ]
    x_row = near(pl.pallas_call(
        rows_kernel,
        out_shape=jax.ShapeDtypeStruct((col_devs * owned, width, LANES), BF16),
        in_specs=[VM] * (runs + 1) + [ANY],
        out_specs=VM,
        compiler_params=params(4),
        cost_estimate=cost(4 << 30, 8 << 20),
    )(own_x, beside, *turned, xcol))
    def shape(*dims, dtype=BF16):
        return jax.ShapeDtypeStruct(dims, dtype)

    def along_y(x, s):
        return near(lax.ppermute(x, "col", [(i, i // runs * runs + (i + s) % runs) for i in range(col_devs)]))

    def along_x(x, s):
        return near(lax.ppermute(x, "row", [(i, (i + 4 * s) % row_devs) for i in range(row_devs)]))

    def call(kernel, out_shape, *args):
        return pl.pallas_call(
            kernel,
            out_shape=out_shape,
            in_specs=[VM] * len(args),
            out_specs=jax.tree.map(lambda _: VM, out_shape),
            compiler_params=params(4),
        )(*args)

    *ring, row_keep, col_keep, core_out = pl.pallas_call(
        block_kernel,
        out_shape=(
            *[shape(2, width, span)] * (runs - 1),
            shape(2, width, span, dtype=F32),
            shape(2 * lines, width, span, dtype=F32),
            shape(2 * lines + 1, width, span),
        ),
        in_specs=[SM, HBM, HBM] + [VM] * 4 + [HBM],
        out_specs=(VM,) * (runs + 2),
        scratch_shapes=[
            pltpu.VMEM((row_devs * owned, width, LANES), BF16),
            pltpu.VMEM((col_devs * owned + 1, width, LANES), F32),
            pltpu.VMEM((row_devs * owned + 1, width, LANES), F32),
        ] + block_scratch,
        compiler_params=params(24),
    )(count, rows, cols, x_row, xcol, xcol_twin, stats, blocks)
    got_core = near(lax.ppermute(core_out, "row", [(i, i ^ 1) for i in range(row_devs)]))
    *line, col_keep, tile = call(
        core_kernel,
        (*[shape(2, width, wide)] * (lines - 1), shape(2, width, span, dtype=F32), shape(width, LANES)),
        core_out, got_core, col_keep,
    )
    line = [along_x(part, s + 1) for s, part in enumerate(line)]
    ring = [along_y(part, s + 1) for s, part in enumerate(ring)]
    tile = call(line_tile_kernel, shape(width, LANES), tile, *line)
    tiles = [along_y(tile, s) for s in range(1, runs)]
    own, col_raw, row_raw = call(
        sums_kernel,
        (shape(width, span, dtype=F32), shape(width, span), shape(width, span)),
        diag_term, col_keep, row_keep, *line, *ring,
    )
    col_out, row_out, tile = call(
        ring_tile_kernel,
        (shape(width, wide), shape(width, wide), shape(width, LANES)),
        tile, *tiles, col_raw, row_raw,
    )
    got_col = near(lax.ppermute(col_out, "row", [(i, i ^ 2) for i in range(row_devs)]))
    got_row = near(lax.ppermute(row_out, "col", [(i, (i + runs) % col_devs) for i in range(col_devs)]))
    across = near(lax.ppermute(tile, ("row", "col"), across_z))
    return pl.pallas_call(
        final_kernel,
        out_shape=(shape(width, span, dtype=F32), shape(width, span)),
        in_specs=[VM] * 7,
        out_specs=(VM, VM),
        compiler_params=params(4),
    )(own, got_col, got_row, tile, across, own_x, precond)


def solution(mesh):
    placed = (
        P(None, ("row", "col")),
        P("row", "col", None, None, None),
        P("row", "col", None),
        P("row", "col", None),
        P("row", "col"),
        P(("row", "col"), None, None),
        P(("row", "col"), None, None),
    )
    return jax.shard_map(
        per_device,
        mesh=mesh,
        in_specs=placed,
        out_specs=(P(None, ("row", "col")), P(None, ("row", "col"))),
        check_vma=False,
    )
```

```python
import functools
import jax
import jax.numpy as jnp
from jax import lax
from jax.experimental import pallas as pl
from jax.experimental.pallas import tpu as pltpu
from jax.sharding import PartitionSpec as P

CHUNK = 32
GROUP = 8
LANES = 128
PARTS = 2
F32 = jnp.float32
BF16 = jnp.bfloat16


def split_tile(xy, xx, width):
    lane = lax.broadcasted_iota(jnp.int32, (width, LANES), 1)
    v = jnp.where(lane % 2 == 0, xy, xx)
    hi = v.astype(BF16).astype(F32)
    mid = (v - hi).astype(BF16).astype(F32)
    low = v - hi - mid
    tile = jnp.where(lane < 2, hi, jnp.where(lane < 4, mid, jnp.where(lane < 6, low, 0.0)))
    return tile.astype(BF16)


def join_tile(tile):
    lane = lax.broadcasted_iota(jnp.int32, tile.shape, 1)
    xy = jnp.sum(jnp.where(lane % 2 == 0, tile, 0.0), axis=1, keepdims=True)
    xx = jnp.sum(jnp.where(lane % 2 == 1, tile, 0.0), axis=1, keepdims=True)
    return xy, xx


def fetch(stiff_ref, buf, sems, count):
    copies = []
    for c in range(stiff_ref.shape[0] // CHUNK):
        here = pl.ds(c * CHUNK, CHUNK)
        copies.append(pltpu.make_async_copy(stiff_ref.at[here], buf.at[here], sems.at[c]))
    for c, copy in enumerate(copies):
        pl.when(c * CHUNK < count)(copy.start)
    return copies


def pair_products(xa, xb, blocks, turned):
    none = jnp.zeros_like(xa)
    x = jnp.concatenate([jnp.concatenate([xa, none], axis=1), jnp.concatenate([none, xb], axis=1)], axis=0)
    if turned:
        b = jnp.concatenate([blocks[0], blocks[1]], axis=1)
        dims = ((1,), (1,))
    else:
        b = blocks.reshape(2 * blocks.shape[1], blocks.shape[2])
        dims = ((1,), (0,))
    out = lax.dot_general(x, b, (dims, ((), ())), preferred_element_type=F32)
    return out[:xa.shape[0]], out[xa.shape[0]:]


def diag_kernel(x_ref, diag_ref, term_ref, stats_ref, near_ref):
    width, span = x_ref.shape
    xy = jnp.zeros((width, LANES), F32)
    xx = jnp.zeros((width, LANES), F32)
    for g in range(span // LANES):
        here = slice(g * LANES, (g + 1) * LANES)
        xg = x_ref[:, here]
        d = diag_ref[g]
        term = lax.dot_general(xg, d, (((1,), (1,)), ((), ())), preferred_element_type=F32)
        term = term + lax.dot_general(xg, d, (((1,), (0,)), ((), ())), preferred_element_type=F32)
        term_ref[:, here] = term
        xf = xg.astype(F32)
        xy = xy + xf * term
        xx = xx + xf * xf
    stats_ref[0] = xy
    stats_ref[1] = xx
    near_ref[...] = x_ref[...]


def rows_kernel(x_ref, z_ref, *refs):
    (*pair_refs, after_ref, x_row) = refs
    owned = x_ref.shape[1] // LANES
    runs = len(pair_refs) + 1
    place = lax.axis_index("col")
    zl = place // runs
    y = place % runs
    for s in range(runs):
        for k in range(2):
            dev = ((zl + k) % 2) * runs + (y + runs - s) % runs
            for t in range(owned):
                here = slice(t * LANES, (t + 1) * LANES)
                piece = (x_ref if k == 0 else z_ref)[:, here] if s == 0 else pair_refs[s - 1][k, :, here]
                x_row[dev * owned + t] = piece


def block_kernel(count_ref, rows_hbm, cols_hbm, x_row, xcol_ref, twin_ref, stats_ref, stiff_ref, *refs):
    (*ring_refs, row_keep, col_keep, core_out, x_col, acc_row, acc_col, buf, rows_ref, cols_ref, sems, index_sems) = refs
    count = count_ref[0, 0]
    index_copies = [
        pltpu.make_async_copy(rows_hbm, rows_ref, index_sems.at[0]),
        pltpu.make_async_copy(cols_hbm, cols_ref, index_sems.at[1]),
    ]
    copies = fetch(stiff_ref, buf, sems, count)
    for copy in index_copies:
        copy.start()
    width, span = xcol_ref.shape[2:]
    owned = span // LANES
    acc_row[...] = jnp.zeros_like(acc_row)
    acc_col[...] = jnp.zeros_like(acc_col)
    place = lax.axis_index("row")
    lines = xcol_ref.shape[0]
    for s in range(lines):
        for k in range(2):
            for twin, ref in enumerate((xcol_ref, twin_ref)):
                dev = (place // 4 + lines - s) % lines * 4 + (place // 2 + k) % 2 * 2 + (place + twin) % 2
                for t in range(owned):
                    x_col[dev * owned + t] = ref[s, k, :, t * LANES:(t + 1) * LANES]
    for copy in index_copies:
        copy.wait()
    for c, copy in enumerate(copies):

        @pl.when(c * CHUNK < count)
        def _():
            copy.wait()
            for h in range(0, CHUNK, GROUP):
                found = []
                for n in range(c * CHUNK + h, c * CHUNK + h + GROUP, 2):
                    i = [rows_ref[n + k] for k in range(2)]
                    j = [cols_ref[n + k] for k in range(2)]
                    to_row = pair_products(x_col[j[0]], x_col[j[1]], buf[n:n + 2], True)
                    to_col = pair_products(x_row[i[0]], x_row[i[1]], buf[n:n + 2], False)
                    for k in range(2):
                        live = n + k < count
                        found.append((acc_row, jnp.where(live, i[k], acc_row.shape[0] - 1), to_row[k]))
                        found.append((acc_col, jnp.where(live, j[k], acc_col.shape[0] - 1), to_col[k]))
                for acc, g, term in found:
                    acc[g] += term

    runs = len(ring_refs) + 1
    place = lax.axis_index("col")
    part = jnp.zeros((width, LANES), F32)
    for s in range(runs):
        for k in range(2):
            dev = (place // runs + k) % 2 * runs + (place + s) % runs
            for t in range(owned):
                here = slice(t * LANES, (t + 1) * LANES)
                a = acc_row[dev * owned + t]
                part = part + a * x_row[dev * owned + t].astype(F32)
                if s == 0:
                    row_keep[k, :, here] = a
                else:
                    ring_refs[s - 1][k, :, here] = a.astype(BF16)
    place = lax.axis_index("row")
    lines = xcol_ref.shape[0]
    for s in range(lines):
        for k in range(2):
            dev = (place // 4 + s) % lines * 4 + (place // 2 + k) % 2 * 2
            for t in range(owned):
                here = slice(t * LANES, (t + 1) * LANES)
                col_keep[2 * s + k, :, here] = acc_col[(dev + place % 2) * owned + t]
                core_out[2 * s + k, :, here] = acc_col[(dev + (place + 1) % 2) * owned + t].astype(BF16)
    xy = jnp.sum(2.0 * part + stats_ref[0], axis=1, keepdims=True)
    xx = jnp.sum(stats_ref[1], axis=1, keepdims=True)
    core_out[2 * lines, :, :LANES] = split_tile(xy, xx, width)
    core_out[2 * lines, :, LANES:] = jnp.zeros((width, span - LANES), BF16)


def tile_sum(first, *more):
    total = first.astype(F32)
    for tile in more:
        total = total + tile.astype(F32)
    return split_tile(*join_tile(total), first.shape[0])


def core_kernel(own_ref, got_ref, keep_ref, *refs):
    (*line_refs, col_keep, tile_ref) = refs
    span = own_ref.shape[2]
    last = keep_ref.shape[0]
    tile = tile_sum(own_ref[last, :, :LANES], got_ref[last, :, :LANES])
    tile_ref[...] = tile
    for n in range(keep_ref.shape[0]):
        s, k = divmod(n, 2)
        for t in range(span // LANES):
            here = slice(t * LANES, (t + 1) * LANES)
            total = keep_ref[n, :, here] + got_ref[n, :, here].astype(F32)
            if s == 0:
                col_keep[k, :, here] = total
            else:
                line_refs[s - 1][k, :, here] = total.astype(BF16)
        if s > 0:
            line_refs[s - 1][k, :, span:] = tile


def line_tile_kernel(tile_ref, *refs):
    *got, out = refs
    span = got[0].shape[2] - LANES
    out[...] = tile_sum(tile_ref[...], *[ref[0, :, span:] for ref in got])


def ring_tile_kernel(*refs):
    *tiles, col_raw, row_raw, col_out, row_out, out = refs
    span = col_raw.shape[1]
    tile = tile_sum(*[ref[...] for ref in tiles])
    out[...] = tile
    for raw, ref in ((col_raw, col_out), (row_raw, row_out)):
        ref[:, :span] = raw[...]
        ref[:, span:] = tile


def sums_kernel(diag_ref, col_keep, row_keep, *refs):
    (*got, own_ref, col_raw, row_raw) = refs
    half = len(got) // 2
    for t in range(own_ref.shape[1] // LANES):
        here = slice(t * LANES, (t + 1) * LANES)
        total = [[keep[k, :, here] for k in range(2)] for keep in (col_keep, row_keep)]
        for g, ref in enumerate(got):
            for k in range(2):
                total[g // half][k] = total[g // half][k] + ref[k, :, here].astype(F32)
        own_ref[:, here] = diag_ref[:, here] + total[0][0] + total[1][0]
        col_raw[:, here] = total[0][1].astype(BF16)
        row_raw[:, here] = total[1][1].astype(BF16)


def final_kernel(own_ref, col_ref, row_ref, tile_ref, across_ref, x_ref, pre_ref, image_hbm, search_hbm,
                 image_ref, search_ref, sems):
    span = own_ref.shape[1]
    quarter = span // PARTS
    copies = []
    for p in range(PARTS):
        for k, (ref, out) in enumerate(((image_ref, image_hbm), (search_ref, search_hbm))):
            here = pl.ds(p * quarter, quarter)
            copies.append(pltpu.make_async_copy(ref.at[:, here], out.at[:, here], sems.at[2 * p + k]))
    for p in range(PARTS):
        for t in range(p * quarter // LANES, (p + 1) * quarter // LANES):
            here = slice(t * LANES, (t + 1) * LANES)
            image_ref[:, here] = own_ref[:, here] + col_ref[:, here].astype(F32) + row_ref[:, here].astype(F32)
        copies[2 * p].start()
    tile = tile_ref[...].astype(F32) + across_ref[...].astype(F32)
    xy, xx = join_tile(tile + col_ref[:, span:].astype(F32) + row_ref[:, span:].astype(F32))
    theta = xy / xx
    for p in range(PARTS):
        for t in range(p * quarter // LANES, (p + 1) * quarter // LANES):
            here = slice(t * LANES, (t + 1) * LANES)
            resid = (image_ref[:, here] - theta * x_ref[:, here].astype(F32)).astype(BF16)
            out = lax.dot_general(resid, pre_ref[t], (((1,), (1,)), ((), ())), preferred_element_type=F32)
            search_ref[:, here] = out.astype(BF16)
        copies[2 * p + 1].start()
    for copy in copies:
        copy.wait()


def pairs_kernel(x_ref, z_ref, h_ref, ring_ref, line_ref):
    for ref, other in ((ring_ref, z_ref), (line_ref, h_ref)):
        ref[0] = x_ref[...]
        ref[1] = other[...]


def stack_kernel(*refs):
    *parts, out = refs
    for s, ref in enumerate(parts):
        out[s] = ref[...]


VM = pl.BlockSpec(memory_space=pltpu.VMEM)
SM = pl.BlockSpec(memory_space=pltpu.SMEM)
ANY = pl.BlockSpec(memory_space=pl.ANY)
HBM = pl.BlockSpec(memory_space=pltpu.HBM)


def near(x):
    return pltpu.with_memory_space_constraint(x, pltpu.VMEM)


def params(mib):
    return pltpu.CompilerParams(vmem_limit_bytes=mib << 20)


def cost(flops, moved):
    return pl.CostEstimate(flops=flops, bytes_accessed=moved, transcendentals=0)


def per_device(vectors, stiffness, block_row, block_col, block_count, diag_blocks, precond):
    width, span = vectors.shape
    owned, block_len, _ = diag_blocks.shape
    slots = stiffness.shape[2]
    row_devs = lax.axis_size("row")
    col_devs = lax.axis_size("col")
    runs = col_devs // 2
    wide = span + LANES
    count = block_count
    rows = pltpu.with_memory_space_constraint(block_row.reshape(slots), pltpu.HBM)
    cols = pltpu.with_memory_space_constraint(block_col.reshape(slots), pltpu.HBM)
    block_scratch = [
        pltpu.VMEM((slots, block_len, block_len), BF16),
        pltpu.SMEM((slots,), jnp.int32),
        pltpu.SMEM((slots,), jnp.int32),
        pltpu.SemaphoreType.DMA((slots // CHUNK,)),
        pltpu.SemaphoreType.DMA((2,)),
    ]
    blocks = pltpu.with_memory_space_constraint(stiffness.reshape(slots, block_len, block_len), pltpu.HBM)

    beside = near(lax.ppermute(vectors, "col", [(i, (i + runs) % col_devs) for i in range(col_devs)]))
    across_z = [
        (r * col_devs + c, (r ^ 2) * col_devs + (c + runs) % col_devs)
        for r in range(row_devs)
        for c in range(col_devs)
    ]
    above = near(lax.ppermute(vectors, "row", [(i, i ^ 2) for i in range(row_devs)]))
    diag_term, stats, own_x = pl.pallas_call(
        diag_kernel,
        out_shape=(
            jax.ShapeDtypeStruct((width, span), F32),
            jax.ShapeDtypeStruct((2, width, LANES), F32),
            jax.ShapeDtypeStruct((width, span), BF16),
        ),
        in_specs=[VM, VM],
        out_specs=(VM, VM, VM),
        compiler_params=params(4),
        cost_estimate=cost(1 << 30, 4 << 20),
    )(vectors, diag_blocks)
    diag_term, stats, own_x = near(diag_term), near(stats), near(own_x)
    lines = row_devs // 4
    pair, line = pl.pallas_call(
        pairs_kernel,
        out_shape=(jax.ShapeDtypeStruct((2, width, span), BF16),) * 2,
        in_specs=[VM, VM, VM],
        out_specs=(VM, VM),
        compiler_params=params(4),
    )(own_x, beside, above)
    pair, line = near(pair), near(line)
    passed = [
        near(lax.ppermute(line, "row", [(i, (i + 4 * s) % row_devs) for i in range(row_devs)])) for s in range(1, lines)
    ]
    xcol = near(pl.pallas_call(
        stack_kernel,
        out_shape=jax.ShapeDtypeStruct((lines, 2, width, span), BF16),
        in_specs=[VM] * lines,
        out_specs=VM,
        compiler_params=params(4),
        cost_estimate=cost(0, 1 << 20),
    )(line, *passed))
    xcol_twin = near(lax.ppermute(xcol, "row", [(i, i ^ 1) for i in range(row_devs)]))
    turned = [
        near(lax.ppermute(pair, "col", [(i, i // runs * runs + (i + s) % runs) for i in range(col_devs)]))
        for s in range(1, runs)
    ]
    x_row = near(pl.pallas_call(
        rows_kernel,
        out_shape=jax.ShapeDtypeStruct((col_devs * owned, width, LANES), BF16),
        in_specs=[VM] * (runs + 1) + [ANY],
        out_specs=VM,
        compiler_params=params(4),
        cost_estimate=cost(4 << 30, 8 << 20),
    )(own_x, beside, *turned, xcol))
    def shape(*dims, dtype=BF16):
        return jax.ShapeDtypeStruct(dims, dtype)

    def along_y(x, s):
        return near(lax.ppermute(x, "col", [(i, i // runs * runs + (i + s) % runs) for i in range(col_devs)]))

    def along_x(x, s):
        return near(lax.ppermute(x, "row", [(i, (i + 4 * s) % row_devs) for i in range(row_devs)]))

    def call(kernel, out_shape, *args):
        return pl.pallas_call(
            kernel,
            out_shape=out_shape,
            in_specs=[VM] * len(args),
            out_specs=jax.tree.map(lambda _: VM, out_shape),
            compiler_params=params(4),
        )(*args)

    *ring, row_keep, col_keep, core_out = pl.pallas_call(
        block_kernel,
        out_shape=(
            *[shape(2, width, span)] * (runs - 1),
            shape(2, width, span, dtype=F32),
            shape(2 * lines, width, span, dtype=F32),
            shape(2 * lines + 1, width, span),
        ),
        in_specs=[SM, HBM, HBM] + [VM] * 4 + [HBM],
        out_specs=(VM,) * (runs + 2),
        scratch_shapes=[
            pltpu.VMEM((row_devs * owned, width, LANES), BF16),
            pltpu.VMEM((col_devs * owned + 1, width, LANES), F32),
            pltpu.VMEM((row_devs * owned + 1, width, LANES), F32),
        ] + block_scratch,
        compiler_params=params(24),
    )(count, rows, cols, x_row, xcol, xcol_twin, stats, blocks)
    got_core = near(lax.ppermute(core_out, "row", [(i, i ^ 1) for i in range(row_devs)]))
    *line, col_keep, tile = call(
        core_kernel,
        (*[shape(2, width, wide)] * (lines - 1), shape(2, width, span, dtype=F32), shape(width, LANES)),
        core_out, got_core, col_keep,
    )
    line = [along_x(part, s + 1) for s, part in enumerate(line)]
    ring = [along_y(part, s + 1) for s, part in enumerate(ring)]
    tile = call(line_tile_kernel, shape(width, LANES), tile, *line)
    tiles = [along_y(tile, s) for s in range(1, runs)]
    own, col_raw, row_raw = call(
        sums_kernel,
        (shape(width, span, dtype=F32), shape(width, span), shape(width, span)),
        diag_term, col_keep, row_keep, *line, *ring,
    )
    col_out, row_out, tile = call(
        ring_tile_kernel,
        (shape(width, wide), shape(width, wide), shape(width, LANES)),
        tile, *tiles, col_raw, row_raw,
    )
    got_col = near(lax.ppermute(col_out, "row", [(i, i ^ 2) for i in range(row_devs)]))
    got_row = near(lax.ppermute(row_out, "col", [(i, (i + runs) % col_devs) for i in range(col_devs)]))
    across = near(lax.ppermute(tile, ("row", "col"), across_z))
    return pl.pallas_call(
        final_kernel,
        out_shape=(shape(width, span, dtype=F32), shape(width, span)),
        in_specs=[VM] * 7,
        out_specs=(HBM, HBM),
        scratch_shapes=[
            pltpu.VMEM((width, span), F32),
            pltpu.VMEM((width, span), BF16),
            pltpu.SemaphoreType.DMA((2 * PARTS,)),
        ],
        compiler_params=params(4),
    )(own, got_col, got_row, tile, across, own_x, precond)


def solution(mesh):
    placed = (
        P(None, ("row", "col")),
        P("row", "col", None, None, None),
        P("row", "col", None),
        P("row", "col", None),
        P("row", "col"),
        P(("row", "col"), None, None),
        P(("row", "col"), None, None),
    )
    return jax.shard_map(
        per_device,
        mesh=mesh,
        in_specs=placed,
        out_specs=(P(None, ("row", "col")), P(None, ("row", "col"))),
        check_vma=False,
    )
```
